256 devices in a mesh: image: 16 (over x, y_lo, core), space: 16 (over z, y_hi).
Axes of the slice: x: 4, y: 4 (y_hi: 2, y_lo: 2; y = y_hi * 2 + y_lo), z: 8, core: 2. Of those that a mesh axis runs over, the one named last changes fastest.
Arguments:
- coords: float32 [32, 3, 131072], P('image', None, 'space'), may hold values from -16 to 16
- ref_coords: float32 [3, 131072], P(None, 'space'), may hold values from -4 to 4
- restraint: float32 [131072], P('space'), may hold values from 0.5 to 5
- atom_types: int32 [131072], P('space'), may hold values from 0 to 63
- well_table: float32 [64], replicated, may hold values from 0.3 to 1.5
- radius_table: float32 [64], replicated, may hold values from 0.4 to 1
- tile_lists: int32 [32, 4, 1024], P('image', None, 'space'), may hold values from 0 to 79
- halo_index: int32 [32, 2, 16384], P('image', None, 'space'), may hold values from 0 to 8191
Outputs:
- neb_force: float32 [32, 3, 131072], P('image', None, 'space')
- energies: float32 [32], P('image')
The draws below stay inside these ranges and needn't reach their ends.
All inputs are finite; a program needn't handle non-finite values.
Results may differ from the reference program's by a relative error of at most 0.0001.
Values sent between devices are 32-bit elements; how exact they have to be, the bound alone decides.
No kernel may reach another device: no remote copies, remote signals or barrier semaphores. Data moves between devices by JAX's collectives and lax.ppermute only.
A program may use at most 64 MiB of HBM per device.

```python
import math
import jax
import jax.numpy as jnp
from jax import lax

ATOMS_DEV = 8192
HALO = 1024
PARTNERS = 4
NTYPES = 64
TILE = 128
NT_EXT = 80
IMAGES = 32
ATOMS = 131072
TILES = 1024
HALOS = 16384
N_SPACE = 16


def common_layout(key):
    position = jnp.arange(ATOMS, dtype=jnp.float32) / ATOMS
    base = jnp.clip(jax.random.normal(jax.random.fold_in(key, 11), (3, ATOMS), jnp.float32), -4.0, 4.0)
    base = base * 0.6 * (1.6 - 0.8 * position)
    path = jnp.clip(jax.random.normal(jax.random.fold_in(key, 12), (3, ATOMS), jnp.float32), -4.0, 4.0)
    spread = jnp.exp(jax.random.uniform(jax.random.fold_in(key, 13), (ATOMS,), jnp.float32, math.log(0.2), math.log(2.0)))
    spread = spread * (1.0 + 2.0 * position) / 2.0
    return (base, path, spread)


def draw_coords(key, part):
    base, path, spread = common_layout(key)
    scales = jnp.exp(jax.random.uniform(jax.random.fold_in(key, 14), (IMAGES, 1, 1), jnp.float32, math.log(0.3), math.log(3.0)))
    noise = jnp.clip(jax.random.normal(jax.random.fold_in(key, 15), (IMAGES, 3, ATOMS), jnp.float32), -4.0, 4.0)
    return base[None] + 0.3 * scales * path[None] * spread + 0.1 * noise * spread


def draw_ref_coords(key, part):
    base, path, spread = common_layout(key)
    return base


def draw_tile_lists(key, part):
    values = jax.random.randint(key, (IMAGES, PARTNERS, TILES), 0, NT_EXT, jnp.int32)
    return values.at[0, 0, 0].set(NT_EXT - 1).at[0, 1, 0].set(0)


def draw_halo_index(key, part):
    values = jax.random.randint(key, (IMAGES, 2, HALOS), 0, ATOMS_DEV, jnp.int32)
    return values.at[0, 0, 0].set(ATOMS_DEV - 1).at[0, 0, 1].set(0)


def set_ends(drawn, own_key, low, largest):
    shape = drawn.shape
    spot = [jax.random.randint(jax.random.fold_in(own_key, axis), (), 0, shape[axis]) for axis in range(len(shape))]
    drawn = drawn.at[tuple(spot)].set(low)
    longest = shape.index(max(shape))
    spot[longest] = (spot[longest] + 1) % shape[longest]
    return drawn.at[tuple(spot)].set(largest)


def block_levels(rng, dims, shards, smallest, top_value):
    gain, own = 1.0, jax.random.fold_in(rng, 6)
    for dim, parts in shards:
        steps = jnp.exp(jax.random.uniform(jax.random.fold_in(own, dim), (parts,), jnp.float32, smallest / len(shards), top_value / len(shards)))
        gain = gain * jnp.repeat(steps, dims[dim] // parts).reshape([-1 if axis == dim else 1 for axis in range(len(dims))])
    return gain


def setup_inputs(seed: int = 0) -> dict:
    key_list = jax.random.split(jax.random.key(seed), 9)
    coords = draw_coords(jax.random.fold_in(key_list[8], 71), 0)
    ref_coords = draw_ref_coords(jax.random.fold_in(key_list[8], 71), 0)
    restraint = jnp.clip(jnp.exp(math.log(5.0) - 2.3025851 * jax.random.uniform(key_list[2], (ATOMS,), jnp.float32) ** block_levels(key_list[2], (ATOMS,), ((0, 16),), -0.2, 0.2)), 0.5, 5.0)
    atom_types = set_ends(jax.random.randint(key_list[3], (ATOMS,), 0, NTYPES), jax.random.fold_in(key_list[3], 1), 0, NTYPES - 1).astype(jnp.int32)
    well_table = jnp.clip(jnp.exp(jax.random.uniform(key_list[4], (NTYPES,), jnp.float32, math.log(0.3), math.log(1.5))), 0.3, 1.5)
    radius_table = jnp.clip(jnp.exp(jax.random.uniform(key_list[5], (NTYPES,), jnp.float32, math.log(0.4), math.log(1.0))), 0.4, 1.0)
    tile_lists = draw_tile_lists(jax.random.fold_in(key_list[8], 71), 0)
    halo_index = draw_halo_index(jax.random.fold_in(key_list[8], 71), 0)
    return {"coords": coords, "ref_coords": ref_coords, "restraint": restraint, "atom_types": atom_types, "well_table": well_table, "radius_table": radius_table, "tile_lists": tile_lists, "halo_index": halo_index}


soft_core = 1.0
spring_k = 2.0
small_eps = 1e-06

def pair_terms(own, partner):
    delta = own[:3, ..., :, None] - partner[:3, ..., None, :]
    dist_sq = lax.optimization_barrier(jnp.sum(delta * delta, axis=0))
    reach = own[4, ..., :, None] + partner[4, ..., None, :]
    reach_sq = reach * reach
    ratio = reach_sq / (dist_sq + soft_core * reach_sq)
    cubed = ratio * ratio * ratio
    strength = own[3, ..., :, None] * partner[3, ..., None, :]
    energy = lax.optimization_barrier(jnp.sum(4.0 * strength * (cubed * cubed - cubed), axis=(-2, -1)))
    coeff = 24.0 * strength * (2.0 * cubed * cubed - cubed) * ratio / reach_sq
    force = lax.optimization_barrier(jnp.sum(coeff[None] * delta, axis=-1))
    return (force, energy)

def reference(coords, ref_coords, restraint, atom_types, well_table, radius_table, tile_lists, halo_index):
    depth_atom = well_table[atom_types]
    radius_atom = radius_table[atom_types]
    tiles_dev = ATOMS_DEV // TILE
    pick_atoms = jax.vmap(lambda source, index: source[:, index])
    pick_tiles = jax.vmap(lambda source, index: source[:, index, :])

    def one_image(inputs):
        position, lists, halos = inputs
        feats = jnp.concatenate([position, depth_atom[None], radius_atom[None]], axis=0)
        slabs = feats.reshape(5, N_SPACE, ATOMS_DEV).transpose(1, 0, 2)
        zero_slab = jnp.zeros((1, 5, ATOMS_DEV), jnp.float32)
        below = jnp.concatenate([zero_slab, slabs[:-1]], axis=0)
        above = jnp.concatenate([slabs[1:], zero_slab], axis=0)
        wanted = halos.reshape(2, N_SPACE, HALO)
        lower = pick_atoms(below, wanted[0])
        upper = pick_atoms(above, wanted[1])
        extended = jnp.concatenate([slabs, lower, upper], axis=2).reshape(N_SPACE, 5, -1, TILE)
        own = slabs.reshape(N_SPACE, 5, tiles_dev, TILE).transpose(1, 0, 2, 3)
        chosen = lists.reshape(PARTNERS, N_SPACE, tiles_dev)

        def add_partner(carry, index):
            partner = pick_tiles(extended, index).transpose(1, 0, 2, 3)
            force, energy = pair_terms(own, partner)
            return ((carry[0] + force, carry[1] + jnp.sum(energy)), None)
        start = (jnp.zeros((3, N_SPACE, tiles_dev, TILE), jnp.float32), jnp.zeros((), jnp.float32))
        (force, energy), _ = lax.scan(add_partner, start, chosen)
        force = force.reshape(3, ATOMS)
        offset = position - ref_coords
        force = force - restraint[None] * offset
        energy = (0.5 * energy + 0.5 * jnp.sum(restraint[None] * offset * offset)) / ATOMS
        return (force, energy)
    forces, energies = lax.map(one_image, (coords, tile_lists, halo_index))
    zero_image = jnp.zeros((1, 3, ATOMS), jnp.float32)
    before = jnp.concatenate([zero_image, coords[:-1]], axis=0)
    after = jnp.concatenate([coords[1:], zero_image], axis=0)
    ahead = after - coords
    behind = coords - before
    ahead_len = jnp.sqrt(lax.optimization_barrier(jnp.sum(ahead * ahead, axis=(1, 2))) + small_eps)[:, None, None]
    behind_len = jnp.sqrt(lax.optimization_barrier(jnp.sum(behind * behind, axis=(1, 2))) + small_eps)[:, None, None]
    tangent = ahead / ahead_len + behind / behind_len
    tan_len = jnp.sqrt(lax.optimization_barrier(jnp.sum(tangent * tangent, axis=(1, 2))) + small_eps)[:, None, None]
    unit = tangent / tan_len
    along = lax.optimization_barrier(jnp.sum(forces * unit, axis=(1, 2)))[:, None, None]
    banded = forces - along * unit + spring_k * (ahead_len - behind_len) * unit
    order = jnp.arange(IMAGES, dtype=jnp.int32)[:, None, None]
    ends = (order == 0) | (order == IMAGES - 1)
    neb_force = jnp.where(ends, forces, banded)
    return (neb_force, energies)
```

```python
import jax
import jax.numpy as jnp
from jax import lax
from jax.experimental import pallas as pl
from jax.experimental.pallas import tpu as pltpu
from jax.sharding import PartitionSpec as P

TILE = 128
PARTNERS = 4
UNROLL = 8
spring_k = 2.0
small_eps = 1e-06
f32, bf16 = jnp.float32, jnp.bfloat16
GROUPS = ((0, 0), (0, 1), (1, 0), (0, 2), (2, 0), (1, 1))
VMEM = pl.BlockSpec(memory_space=pltpu.VMEM)
SMEM = pl.BlockSpec(memory_space=pltpu.SMEM)


def lanes(tile):
    return pl.ds(pl.multiple_of(tile * TILE, TILE), TILE)


def pieces(v):
    first = v.astype(bf16).astype(f32)
    rest = v - first
    second = rest.astype(bf16).astype(f32)
    return first, second, (rest - second).astype(bf16).astype(f32)


def rows_of(shape):
    return lax.broadcasted_iota(jnp.int32, shape, 0)


def streamed_features(x3, depth, radius):
    row = rows_of((8, TILE))
    squares = x3 * x3
    rr = radius * radius
    norm = squares[0:1] + squares[1:2] + squares[2:3] + rr
    cut = pieces(jnp.concatenate([x3, radius, norm, norm, rr, rr], axis=0))
    ones = [jnp.where((row == 5) | (row == 7), 1.0, c) for c in cut]
    streamed = jnp.concatenate([ones[a] for a, _ in GROUPS], axis=0).astype(bf16)
    streamed = jnp.concatenate([streamed, jnp.zeros((80, TILE), bf16)], axis=0)
    moved = jnp.concatenate([depth, depth * x3], axis=0)
    p1, p2, p3 = pieces(jnp.concatenate([moved, moved], axis=0))
    weights = jnp.concatenate(
        [jnp.where(row < 4, p1, p2), jnp.where(row < 4, p3, 0.0)], axis=0
    ).astype(bf16)
    return cut, streamed, weights


def held_features(cut):
    row = rows_of((8, TILE))
    blocks = []
    for a, b in GROUPS:
        own = 1.0 if (a, b) in ((0, 0), (0, 1), (0, 2)) else 0.0
        other = 1.0 if (a, b) in ((0, 0), (1, 0), (2, 0)) else 0.0
        scale_d = jnp.where(row < 3, -2.0, jnp.where(row == 3, 2.0, jnp.where(row == 5, own, 0.0)))
        scale_r = jnp.where(row == 3, 2.0, jnp.where(row == 7, own, 0.0))
        dist = cut[b] * scale_d + jnp.where(row == 4, other, 0.0)
        reach = cut[b] * scale_r + jnp.where(row == 6, other, 0.0)
        blocks.append(jnp.concatenate([dist, reach], axis=1))
    held = jnp.concatenate(blocks, axis=0).astype(bf16)
    return jnp.concatenate([held, jnp.zeros((80, 2 * TILE), bf16)], axis=0)


def pair_kernel(
    lists, sides, coords, below, above, types, tables, hidx, ref, restr, prev, nxt,
    force, sums,
    halo_x, depth_s, radius_s, a_s, b_s, p_s, acc_s,
):
    images = coords.shape[0]
    own_tiles = types.shape[0]
    halo_tiles = halo_x.shape[2]
    side_tiles = halo_tiles // 2
    take = lambda src, idx: jnp.take_along_axis(src, idx, axis=1, mode="promise_in_bounds")
    wells = jnp.broadcast_to(tables[0:1], (8, TILE))
    radii = jnp.broadcast_to(tables[1:2], (8, TILE))
    for b in range(own_tiles // 8):
        kind = types[8 * b : 8 * b + 8]
        for m in range(images):
            depth_s[m, 8 * b : 8 * b + 8] = take(wells, kind)
            radius_s[m, 8 * b : 8 * b + 8] = take(radii, kind)

    for side, source in enumerate((below, above)):
        low, high = [], []
        for m in range(images):
            idx = jnp.concatenate(
                [hidx[m, side : side + 1, q * TILE : (q + 1) * TILE] for q in range(side_tiles)],
                axis=0,
            )
            low.append(idx & (TILE - 1))
            high.append(idx >> 7)

        def gather_row(r, carry):
            chunk = source[:, lanes(r)]
            out = []
            for m in range(images):
                hit = high[m] == r
                for c, row in enumerate((3 * m, 3 * m + 1, 3 * m + 2, 3 * images)):
                    wide = jnp.broadcast_to(chunk[row : row + 1], (8, TILE))
                    out.append(jnp.where(hit, take(wide, low[m]), carry[4 * m + c]))
            return tuple(out)

        zero = jnp.zeros((8, TILE), f32)
        found = lax.fori_loop(0, own_tiles, gather_row, (zero,) * (4 * images), unroll=4)
        inside = sides[side].astype(f32)
        for m in range(images):
            for c in range(3):
                halo_x[m, c, side * side_tiles : (side + 1) * side_tiles] = found[4 * m + c]
            kind = found[4 * m + 3].astype(jnp.int32)
            spot = slice(own_tiles + side * side_tiles, own_tiles + (side + 1) * side_tiles)
            depth_s[m, spot] = take(wells, kind) * inside
            radius_s[m, spot] = take(radii, kind)

    eye = (rows_of((TILE, TILE)) == lax.broadcasted_iota(jnp.int32, (TILE, TILE), 1)).astype(bf16)

    def store_tiles(m, first, made):
        for n in range(0, len(made), 2):
            pair = jnp.concatenate([made[n][1], made[n + 1][1]], axis=0)
            turned = lax.dot_general(
                eye, pair, (((1,), (1,)), ((), ())), preferred_element_type=f32
            ).astype(bf16)
            for h in range(2):
                a_s[m, first + n + h] = turned[:, h * TILE : (h + 1) * TILE]
                p_s[m, first + n + h] = made[n + h][2]

    centers = []
    for m in range(images):
        total = coords[m, :, 0:TILE]
        for t in range(1, own_tiles):
            total = total + coords[m, :, t * TILE : (t + 1) * TILE]
        center = jnp.sum(total, axis=1, keepdims=True) * (1.0 / (own_tiles * TILE))
        center = jnp.broadcast_to(center, (3, TILE))
        centers.append(center)

        def build_own(n, carry):
            made = []
            for h in range(4):
                t = 4 * n + h
                x3 = coords[m, :, lanes(t)] - center
                made.append(streamed_features(x3, depth_s[m, pl.ds(t, 1)], radius_s[m, pl.ds(t, 1)]))
                b_s[m, t] = held_features(made[-1][0])
            store_tiles(m, 4 * n, made)
            return carry

        lax.fori_loop(0, own_tiles // 4, build_own, 0)

        def build_halo(n, carry):
            made = []
            for h in range(4):
                t = 4 * n + h
                x3 = jnp.concatenate([halo_x[m, c, pl.ds(t, 1)] for c in range(3)], axis=0) - center
                q = own_tiles + t
                made.append(streamed_features(x3, depth_s[m, pl.ds(q, 1)], radius_s[m, pl.ds(q, 1)]))
            store_tiles(m, own_tiles + 4 * n, made)
            return carry

        lax.fori_loop(0, halo_tiles // 4, build_halo, 0)

    acc_s[...] = jnp.zeros_like(acc_s)
    for m in range(images):
        center = centers[m]

        def one_tile(t, carry):
            held = b_s[m, t]
            acc = jnp.zeros((16, 2 * TILE), f32)
            for k in range(PARTNERS):
                p = lists[m, k, t]
                both = jnp.dot(a_s[m, p], held, preferred_element_type=f32)
                reach = both[:, TILE:]
                inv = pltpu.reciprocal(both[:, :TILE], approx=True)
                ratio = reach * inv
                cubed = ratio * ratio * ratio
                sixth = cubed * cubed
                energy = sixth - cubed
                coeff = (energy + sixth) * inv
                high = coeff.astype(bf16)
                low = (coeff - high.astype(f32)).astype(bf16)
                left = jnp.concatenate([high, low], axis=0)
                right = jnp.concatenate([energy.astype(bf16), jnp.zeros((TILE, TILE), bf16)], axis=0)
                weights = p_s[m, p]
                acc += jnp.dot(
                    jnp.concatenate([weights, weights], axis=1),
                    jnp.concatenate([left, right], axis=1),
                    preferred_element_type=f32,
                )
            depth = depth_s[m, pl.ds(t, 1)]
            at = lanes(t)
            x = coords[m, :, at]
            joined = acc[0:4] + acc[4:8] + acc[8:12]
            moved = (x - center) * joined[0:1, :TILE] - joined[1:4, :TILE]
            offset = x - ref[:, at]
            pull = restr[:, at] * offset
            total = 24.0 * depth * moved - pull
            force[m, :, at] = total
            if m == 0:
                before, after = prev[:, at], coords[1, :, at]
            else:
                before, after = coords[0, :, at], nxt[:, at]
            ahead, behind = after - x, x - before
            both_ways, bend = ahead + behind, ahead - behind
            acc_s[m, 0] += both_ways * both_ways
            acc_s[m, 1] += both_ways * bend
            acc_s[m, 2] += bend * bend
            acc_s[m, 3] += total * both_ways
            acc_s[m, 4] += total * bend
            acc_s[m, 5] += 0.5 * pull * offset
            acc_s[m, 5, 0:1] += 2.0 * depth * joined[0:1, TILE:]
            return carry

        lax.fori_loop(0, own_tiles, one_tile, 0, unroll=UNROLL)

    line = [jnp.sum(acc_s[m, n], axis=0, keepdims=True) for m in range(images) for n in range(6)]
    line = line + [jnp.zeros_like(line[0])] * (16 - len(line))
    row, lane = rows_of((16, 16)), lax.broadcasted_iota(jnp.int32, (16, 16), 1)
    totals = jnp.sum(jnp.concatenate(line, axis=0), axis=1, keepdims=True)
    totals = jnp.sum(jnp.where(row == lane, totals, 0.0), axis=0, keepdims=True)
    sums[...] = jnp.broadcast_to(totals, (16, 16))


def band_kernel(ends, shares, force, coords, prev, nxt, out, energies):
    total = jnp.sum(shares[...], axis=0, keepdims=True)
    atoms = 16 * coords.shape[2]
    for m in range(coords.shape[0]):
        s_sq, cross, b_sq, f_s, f_b, energy = [
            total[:, 6 * m + n : 6 * m + n + 1] for n in range(6)
        ]
        energies[m] = (energy / atoms)[0, 0]
        base = 0.25 * (s_sq + b_sq) + small_eps
        ahead_sq, behind_sq = base + 0.5 * cross, base - 0.5 * cross
        ahead_len, behind_len = jnp.sqrt(ahead_sq), jnp.sqrt(behind_sq)
        inverse_sum = 1.0 / ahead_len + 1.0 / behind_len
        alpha = 0.5 * inverse_sum
        beta = -0.5 * cross / (ahead_sq * behind_sq * inverse_sum)
        tan_sq = alpha * alpha * s_sq + 2.0 * alpha * beta * cross + beta * beta * b_sq
        tan_len = jnp.sqrt(jnp.maximum(tan_sq, 0.0) + small_eps)
        along = (alpha * f_s + beta * f_b) / tan_len
        stretch = cross / (ahead_len + behind_len)
        gain = (spring_k * stretch - along) / tan_len
        gain = jnp.where(ends[m] == 1, 0.0, gain)
        for_s, for_b = gain * alpha, gain * beta
        for_s = jnp.broadcast_to(for_s, (3, TILE))
        for_b = jnp.broadcast_to(for_b, (3, TILE))
        for t in range(coords.shape[2] // TILE):
            at = slice(t * TILE, (t + 1) * TILE)
            x = coords[m, :, at]
            before = prev[:, at] if m == 0 else coords[0, :, at]
            after = nxt[:, at] if m == 1 else coords[1, :, at]
            ahead, behind = after - x, x - before
            out[m, :, at] = force[m, :, at] + for_s * (ahead + behind) + for_b * (ahead - behind)


def ring(axis, step):
    n = lax.axis_size(axis)
    return [(i, (i + step) % n) for i in range(n)]


def body(
    coords, ref_coords, restraint, atom_types, well_table, radius_table, tile_lists, halo_index
):
    images, _, atoms = coords.shape
    tiles = atoms // TILE
    halo_tiles = 2 * halo_index.shape[2] // TILE
    slab, slabs = lax.axis_index("space"), lax.axis_size("space")
    feats = jnp.concatenate(
        [coords.reshape(3 * images, atoms), atom_types.astype(f32)[None]], axis=0
    )
    below = lax.ppermute(feats, "space", ring("space", 1))
    above = lax.ppermute(feats, "space", ring("space", -1))
    prev = lax.ppermute(coords[images - 1], "image", ring("image", 1))
    nxt = lax.ppermute(coords[0], "image", ring("image", -1))
    sides = jnp.stack([slab > 0, slab < slabs - 1]).astype(jnp.int32)
    tables = jnp.pad(
        jnp.stack([well_table, radius_table]), ((0, 0), (0, TILE - well_table.shape[0]))
    )
    tiles_ext = tiles + halo_tiles
    force, sums = pl.pallas_call(
        pair_kernel,
        out_shape=(
            jax.ShapeDtypeStruct((images, 3, atoms), f32),
            jax.ShapeDtypeStruct((16, 16), f32),
        ),
        in_specs=[SMEM, SMEM] + [VMEM] * 10,
        out_specs=(VMEM, VMEM),
        scratch_shapes=[
            pltpu.VMEM((images, 3, halo_tiles, TILE), f32),
            pltpu.VMEM((images, tiles_ext, TILE), f32),
            pltpu.VMEM((images, tiles_ext, TILE), f32),
            pltpu.VMEM((images, tiles_ext, TILE, TILE), bf16),
            pltpu.VMEM((images, tiles, TILE, 2 * TILE), bf16),
            pltpu.VMEM((images, tiles_ext, 16, TILE), bf16),
            pltpu.VMEM((images, 6, 3, TILE), f32),
        ],
        compiler_params=pltpu.CompilerParams(vmem_limit_bytes=40 << 20),
        name="pair",
    )(
        tile_lists, sides, coords, below, above, atom_types.reshape(tiles, TILE), tables,
        halo_index, ref_coords, restraint[None], prev, nxt,
    )
    shares = lax.all_to_all(sums, "space", 0, 0, tiled=True)
    image = lax.axis_index("image") * images + jnp.arange(images, dtype=jnp.int32)
    ends = ((image == 0) | (image == images * lax.axis_size("image") - 1)).astype(jnp.int32)
    return pl.pallas_call(
        band_kernel,
        out_shape=(
            jax.ShapeDtypeStruct((images, 3, atoms), f32),
            jax.ShapeDtypeStruct((images,), f32),
        ),
        in_specs=[SMEM] + [VMEM] * 5,
        out_specs=(VMEM, SMEM),
        name="band",
    )(ends, shares, force, coords, prev, nxt)


def solution(mesh):
    in_specs = (
        P("image", None, "space"),
        P(None, "space"),
        P("space"),
        P("space"),
        P(),
        P(),
        P("image", None, "space"),
        P("image", None, "space"),
    )
    out_specs = (P("image", None, "space"), P("image"))
    return jax.shard_map(body, mesh=mesh, in_specs=in_specs, out_specs=out_specs, check_vma=False)
```

```python
import jax
import jax.numpy as jnp
from jax import lax
from jax.experimental import pallas as pl
from jax.experimental.pallas import tpu as pltpu
from jax.sharding import PartitionSpec as P

TILE = 128
PARTNERS = 4
UNROLL = 8
spring_k = 2.0
small_eps = 1e-06
f32, bf16 = jnp.float32, jnp.bfloat16
GROUPS = ((0, 0), (0, 1), (1, 0), (0, 2), (2, 0), (1, 1))
VMEM = pl.BlockSpec(memory_space=pltpu.VMEM)
SMEM = pl.BlockSpec(memory_space=pltpu.SMEM)


def lanes(tile):
    return pl.ds(pl.multiple_of(tile * TILE, TILE), TILE)


def pieces(v):
    first = v.astype(bf16).astype(f32)
    rest = v - first
    second = rest.astype(bf16).astype(f32)
    return first, second, (rest - second).astype(bf16).astype(f32)


def rows_of(shape):
    return lax.broadcasted_iota(jnp.int32, shape, 0)


def streamed_features(x3, depth, radius):
    row = rows_of((8, TILE))
    squares = x3 * x3
    rr = radius * radius
    norm = squares[0:1] + squares[1:2] + squares[2:3] + rr
    cut = pieces(jnp.concatenate([x3, radius, norm, norm, rr, rr], axis=0))
    ones = [jnp.where((row == 5) | (row == 7), 1.0, c) for c in cut]
    streamed = jnp.concatenate([ones[a] for a, _ in GROUPS], axis=0).astype(bf16)
    streamed = jnp.concatenate([streamed, jnp.zeros((80, TILE), bf16)], axis=0)
    moved = jnp.concatenate([depth, depth * x3], axis=0)
    p1, p2, p3 = pieces(jnp.concatenate([moved, moved], axis=0))
    weights = jnp.concatenate(
        [jnp.where(row < 4, p1, p2), jnp.where(row < 4, p3, 0.0)], axis=0
    ).astype(bf16)
    return cut, streamed, weights


def held_features(cut):
    row = rows_of((8, TILE))
    blocks = []
    for a, b in GROUPS:
        own = 1.0 if (a, b) in ((0, 0), (0, 1), (0, 2)) else 0.0
        other = 1.0 if (a, b) in ((0, 0), (1, 0), (2, 0)) else 0.0
        scale_d = jnp.where(row < 3, -2.0, jnp.where(row == 3, 2.0, jnp.where(row == 5, own, 0.0)))
        scale_r = jnp.where(row == 3, 2.0, jnp.where(row == 7, own, 0.0))
        dist = cut[b] * scale_d + jnp.where(row == 4, other, 0.0)
        reach = cut[b] * scale_r + jnp.where(row == 6, other, 0.0)
        blocks.append(jnp.concatenate([dist, reach], axis=1))
    held = jnp.concatenate(blocks, axis=0).astype(bf16)
    return jnp.concatenate([held, jnp.zeros((80, 2 * TILE), bf16)], axis=0)


def store_tiles(a_out, p_out, first, made):
    eye = (rows_of((TILE, TILE)) == lax.broadcasted_iota(jnp.int32, (TILE, TILE), 1)).astype(bf16)
    for n in range(0, len(made), 2):
        pair = jnp.concatenate([made[n][1], made[n + 1][1]], axis=0)
        turned = lax.dot_general(
            eye, pair, (((1,), (1,)), ((), ())), preferred_element_type=f32
        ).astype(bf16)
        for h in range(2):
            a_out[first + n + h] = turned[:, h * TILE : (h + 1) * TILE]
            p_out[first + n + h] = made[n + h][2]


def take(src, idx):
    return jnp.take_along_axis(src, idx, axis=1, mode="promise_in_bounds")


def pair_sums(order, count, lists, a, b, p, join, own_tiles, tiles_ext):
    def step(n, carry):
        for h in range(UNROLL):
            u = order[n * UNROLL + h]
            m = u // own_tiles
            t = u - m * own_tiles
            held = b[u]
            acc = jnp.zeros((16, 2 * TILE), f32)
            for k in range(PARTNERS):
                q = m * tiles_ext + lists[m, k, t]
                both = jnp.dot(a[q], held, preferred_element_type=f32)
                reach = both[:, TILE:]
                inv = pltpu.reciprocal(both[:, :TILE], approx=True)
                ratio = reach * inv
                cubed = ratio * ratio * ratio
                sixth = cubed * cubed
                energy = sixth - cubed
                coeff = (energy + sixth) * inv
                high = coeff.astype(bf16)
                low = (coeff - high.astype(f32)).astype(bf16)
                left = jnp.concatenate([high, low], axis=0)
                right = jnp.concatenate([energy.astype(bf16), jnp.zeros((TILE, TILE), bf16)], axis=0)
                weights = p[q]
                acc += jnp.dot(
                    jnp.concatenate([weights, weights], axis=1),
                    jnp.concatenate([left, right], axis=1),
                    preferred_element_type=f32,
                )
            joined = acc[0:4] + acc[4:8] + acc[8:12]
            join[u] = jnp.concatenate([joined[:, :TILE], joined[:, TILE:]], axis=0)
        return carry

    lax.fori_loop(0, (count + UNROLL - 1) // UNROLL, step, 0)


def own_kernel(
    lists, place, coords, types, tables,
    a, b, p, join, center, order, count,
    near, depth_s, radius_s,
):
    images = coords.shape[1]
    own_tiles = types.shape[0]
    tiles_ext = a.shape[0] // images
    wells = jnp.broadcast_to(tables[0:1], (8, TILE))
    radii = jnp.broadcast_to(tables[1:2], (8, TILE))
    for n in range(own_tiles // 8):
        kind = types[8 * n : 8 * n + 8]
        depth_s[8 * n : 8 * n + 8] = take(wells, kind)
        radius_s[8 * n : 8 * n + 8] = take(radii, kind)
    for c in range(3):
        total = coords[c, :, 0:TILE]
        for t in range(1, own_tiles):
            total = total + coords[c, :, t * TILE : (t + 1) * TILE]
        middle = jnp.sum(total, axis=1, keepdims=True) * (1.0 / (own_tiles * TILE))
        for m in range(images):
            center[m, c : c + 1] = jnp.broadcast_to(middle[m : m + 1], (1, TILE))

    n_near, n_far = jnp.int32(0), jnp.int32(0)
    for m in range(images):
        middle = center[m, 0:3]

        def build(n, carry):
            n_near, n_far = carry
            made = []
            for h in range(8):
                t = 8 * n + h
                u = m * own_tiles + t
                x3 = jnp.concatenate([coords[c, m : m + 1, lanes(t)] for c in range(3)], axis=0)
                made.append(
                    streamed_features(x3 - middle, depth_s[pl.ds(t, 1)], radius_s[pl.ds(t, 1)])
                )
                b[u] = held_features(made[-1][0])
                last = lists[m, 0, t]
                for k in range(1, PARTNERS):
                    last = jnp.maximum(last, lists[m, k, t])
                inside = (last < own_tiles).astype(jnp.int32)
                near[n_near] = u
                order[n_far] = u
                n_near = n_near + inside
                n_far = n_far + (1 - inside)
            store_tiles(a, p, m * tiles_ext + 8 * n, made)
            return n_near, n_far

        n_near, n_far = lax.fori_loop(0, own_tiles // 8, build, (n_near, n_far))
    last_near = near[jnp.maximum(n_near - 1, 0)]
    last_far = order[jnp.maximum(n_far - 1, 0)]
    for h in range(UNROLL):
        near[n_near + h] = last_near
        order[n_far + h] = last_far
    count[0] = n_far
    pair_sums(near, n_near, lists, a, b, p, join, own_tiles, tiles_ext)


def rest_kernel(
    lists, place, order, count, coords, below, above, types, tables, hidx, ref, restr, prev, nxt,
    center, b, a_in, p_in, join_in,
    force, sums, a, p, join,
    halo_x, depth_s, radius_s, own_depth,
):
    images = coords.shape[1]
    own_tiles = types.shape[0]
    tiles_ext = a.shape[0] // images
    halo_tiles = tiles_ext - own_tiles
    side_tiles = halo_tiles // 2
    wells = jnp.broadcast_to(tables[0:1], (8, TILE))
    radii = jnp.broadcast_to(tables[1:2], (8, TILE))
    for n in range(own_tiles // 8):
        own_depth[8 * n : 8 * n + 8] = take(wells, types[8 * n : 8 * n + 8])

    for side, source in enumerate((below, above)):
        low, high = [], []
        for m in range(images):
            idx = jnp.concatenate(
                [hidx[m, side : side + 1, q * TILE : (q + 1) * TILE] for q in range(side_tiles)],
                axis=0,
            )
            low.append(idx & (TILE - 1))
            high.append(idx >> 7)

        def gather_row(r, carry):
            out = []
            for m in range(images):
                hit = high[m] == r
                for c in range(4):
                    wide = jnp.broadcast_to(source[c, m : m + 1, lanes(r)], (8, TILE))
                    out.append(jnp.where(hit, take(wide, low[m]), carry[4 * m + c]))
            return tuple(out)

        zero = jnp.zeros((8, TILE), f32)
        found = lax.fori_loop(0, own_tiles, gather_row, (zero,) * (4 * images), unroll=8)
        inside = place[side].astype(f32)
        spot = slice(side * side_tiles, (side + 1) * side_tiles)
        for m in range(images):
            for c in range(3):
                halo_x[m, c, spot] = found[4 * m + c]
            kind = found[4 * m + 3].astype(jnp.int32)
            depth_s[m, spot] = take(wells, kind) * inside
            radius_s[m, spot] = take(radii, kind)

    for m in range(images):
        middle = center[m, 0:3]

        def build(n, carry):
            made = []
            for h in range(8):
                t = 8 * n + h
                x3 = jnp.concatenate([halo_x[m, c, pl.ds(t, 1)] for c in range(3)], axis=0)
                made.append(
                    streamed_features(
                        x3 - middle, depth_s[m, pl.ds(t, 1)], radius_s[m, pl.ds(t, 1)]
                    )
                )
            store_tiles(a, p, m * tiles_ext + own_tiles + 8 * n, made)
            return carry

        lax.fori_loop(0, halo_tiles // 8, build, 0)

    pair_sums(order, count[0], lists, a, b, p, join, own_tiles, tiles_ext)

    def finish(n, carry):
        carry = list(carry)
        for h in range(4):
            t = 4 * n + h
            at = lanes(t)
            depth = own_depth[pl.ds(t, 1)]
            stiff = restr[:, at]
            rows = [join[m * own_tiles + t] for m in range(images)]
            weight = jnp.concatenate([r[0:1] for r in rows], axis=0)
            carry[5] += 2.0 * depth * jnp.concatenate([r[4:5] for r in rows], axis=0)
            for c in range(3):
                x = coords[c, :, at]
                middle = jnp.concatenate([center[m, c : c + 1] for m in range(images)], axis=0)
                moved = jnp.concatenate([r[1 + c : 2 + c] for r in rows], axis=0)
                offset = x - ref[c : c + 1, at]
                pull = stiff * offset
                total = 24.0 * depth * ((x - middle) * weight - moved) - pull
                force[c, :, at] = total
                before = jnp.concatenate([prev[c, :, at], x[0:1]], axis=0)
                after = jnp.concatenate([x[1:2], nxt[c, :, at]], axis=0)
                ahead, behind = after - x, x - before
                both_ways, bend = ahead + behind, ahead - behind
                carry[0] += both_ways * both_ways
                carry[1] += both_ways * bend
                carry[2] += bend * bend
                carry[3] += total * both_ways
                carry[4] += total * bend
                carry[5] += 0.5 * pull * offset
        return tuple(carry)

    zero = jnp.zeros((images, TILE), f32)
    line = lax.fori_loop(0, own_tiles // 4, finish, (zero,) * 6)
    line = jnp.concatenate(list(line) + [jnp.zeros((16 - 6 * images, TILE), f32)], axis=0)
    row, lane = rows_of((16, 16)), lax.broadcasted_iota(jnp.int32, (16, 16), 1)
    totals = jnp.sum(line, axis=1, keepdims=True)
    totals = jnp.sum(jnp.where(row == lane, totals, 0.0), axis=0, keepdims=True)
    sums[...] = jnp.broadcast_to(totals, (16, 16))


def band_kernel(place, shares, force, coords, prev, nxt, out, energies):
    total = jnp.sum(shares[...], axis=0, keepdims=True)
    images, atoms = coords.shape[1], coords.shape[2]
    parts = []
    for m in range(images):
        s_sq, cross, b_sq, f_s, f_b, energy = [
            total[:, images * n + m : images * n + m + 1] for n in range(6)
        ]
        energies[m] = (energy / (16 * atoms))[0, 0]
        base = 0.25 * (s_sq + b_sq) + small_eps
        ahead_sq, behind_sq = base + 0.5 * cross, base - 0.5 * cross
        ahead_len, behind_len = jnp.sqrt(ahead_sq), jnp.sqrt(behind_sq)
        inverse_sum = 1.0 / ahead_len + 1.0 / behind_len
        alpha = 0.5 * inverse_sum
        beta = -0.5 * cross / (ahead_sq * behind_sq * inverse_sum)
        tan_sq = alpha * alpha * s_sq + 2.0 * alpha * beta * cross + beta * beta * b_sq
        tan_len = jnp.sqrt(jnp.maximum(tan_sq, 0.0) + small_eps)
        along = (alpha * f_s + beta * f_b) / tan_len
        stretch = cross / (ahead_len + behind_len)
        gain = (spring_k * stretch - along) / tan_len
        gain = jnp.where(place[2 + m] == 1, 0.0, gain)
        parts.append((gain * alpha, gain * beta))
    for_s = jnp.concatenate([jnp.broadcast_to(q[0], (1, TILE)) for q in parts], axis=0)
    for_b = jnp.concatenate([jnp.broadcast_to(q[1], (1, TILE)) for q in parts], axis=0)
    for t in range(atoms // TILE):
        at = slice(t * TILE, (t + 1) * TILE)
        for c in range(3):
            x = coords[c, :, at]
            before = jnp.concatenate([prev[c, :, at], x[0:1]], axis=0)
            after = jnp.concatenate([x[1:2], nxt[c, :, at]], axis=0)
            ahead, behind = after - x, x - before
            out[c, :, at] = force[c, :, at] + for_s * (ahead + behind) + for_b * (ahead - behind)


def ring(axis, step):
    n = lax.axis_size(axis)
    return [(i, (i + step) % n) for i in range(n)]


def shape(dims, dtype=f32):
    return jax.ShapeDtypeStruct(dims, dtype)


def params(mib, **more):
    return dict(compiler_params=pltpu.CompilerParams(vmem_limit_bytes=mib << 20), **more)


def body(
    coords, ref_coords, restraint, atom_types, well_table, radius_table, tile_lists, halo_index
):
    images, _, atoms = coords.shape
    tiles = atoms // TILE
    tiles_ext = tiles + 2 * halo_index.shape[2] // TILE
    slab, slabs = lax.axis_index("space"), lax.axis_size("space")
    coords = coords.transpose(1, 0, 2)
    types = atom_types.reshape(tiles, TILE)
    kinds = jnp.broadcast_to(atom_types.astype(f32), (1, images, atoms))
    feats = jnp.concatenate([coords, kinds], axis=0)
    below = lax.ppermute(feats, "space", ring("space", 1))
    above = lax.ppermute(feats, "space", ring("space", -1))
    prev = lax.ppermute(coords[:, images - 1 :], "image", ring("image", 1))
    nxt = lax.ppermute(coords[:, :1], "image", ring("image", -1))
    image, ranks = lax.axis_index("image"), lax.axis_size("image")
    place = [slab > 0, slab < slabs - 1, image == 0, image == ranks - 1]
    place = jnp.stack(place).astype(jnp.int32)
    tables = jnp.pad(
        jnp.stack([well_table, radius_table]), ((0, 0), (0, TILE - well_table.shape[0]))
    )
    own = images * tiles
    a, b, p, join, center, order, count = pl.pallas_call(
        own_kernel,
        out_shape=(
            shape((images * tiles_ext, TILE, TILE), bf16),
            shape((own, TILE, 2 * TILE), bf16),
            shape((images * tiles_ext, 16, TILE), bf16),
            shape((own, 8, TILE)),
            shape((images, 8, TILE)),
            shape((own + UNROLL,), jnp.int32),
            shape((1,), jnp.int32),
        ),
        in_specs=[SMEM] * 2 + [VMEM] * 3,
        out_specs=(VMEM,) * 5 + (SMEM,) * 2,
        scratch_shapes=[
            pltpu.SMEM((own + UNROLL,), jnp.int32),
            pltpu.VMEM((tiles, TILE), f32),
            pltpu.VMEM((tiles, TILE), f32),
        ],
        cost_estimate=pl.CostEstimate(flops=60 * 10**9, bytes_accessed=10**6, transcendentals=0),
        name="own",
        **params(16),
    )(tile_lists, place, coords, types, tables)
    force, sums, *_ = pl.pallas_call(
        rest_kernel,
        out_shape=(
            shape((3, images, atoms)),
            shape((16, 16)),
            shape(a.shape, bf16),
            shape(p.shape, bf16),
            shape(join.shape),
        ),
        in_specs=[SMEM] * 4 + [VMEM] * 15,
        out_specs=(VMEM,) * 5,
        input_output_aliases={16: 2, 17: 3, 18: 4},
        scratch_shapes=[
            pltpu.VMEM((images, 3, tiles_ext - tiles, TILE), f32),
            pltpu.VMEM((images, tiles_ext - tiles, TILE), f32),
            pltpu.VMEM((images, tiles_ext - tiles, TILE), f32),
            pltpu.VMEM((tiles, TILE), f32),
        ],
        name="rest",
        **params(16),
    )(
        tile_lists, place, order, count, coords, below, above, types, tables, halo_index,
        ref_coords, restraint[None], prev, nxt, center, b, a, p, join,
    )
    shares = lax.all_to_all(sums, "space", 0, 0, tiled=True)
    out, energies = pl.pallas_call(
        band_kernel,
        out_shape=(shape((3, images, atoms)), shape((images,))),
        in_specs=[SMEM] + [VMEM] * 5,
        out_specs=(VMEM, SMEM),
        name="band",
        **params(8),
    )(place, shares, force, coords, prev, nxt)
    return out.transpose(1, 0, 2), energies


def solution(mesh):
    in_specs = (
        P("image", None, "space"),
        P(None, "space"),
        P("space"),
        P("space"),
        P(),
        P(),
        P("image", None, "space"),
        P("image", None, "space"),
    )
    out_specs = (P("image", None, "space"), P("image"))
    return jax.shard_map(body, mesh=mesh, in_specs=in_specs, out_specs=out_specs, check_vma=False)
```

```python
import jax
import jax.numpy as jnp
from jax import lax
from jax.experimental import pallas as pl
from jax.experimental.pallas import tpu as pltpu
from jax.sharding import PartitionSpec as P

TILE = 128
PARTNERS = 4
UNROLL = 16
spring_k = 2.0
small_eps = 1e-06
f32, bf16 = jnp.float32, jnp.bfloat16
GROUPS = ((0, 0), (0, 1), (1, 0), (0, 2), (2, 0), (1, 1))
VMEM = pl.BlockSpec(memory_space=pltpu.VMEM)
SMEM = pl.BlockSpec(memory_space=pltpu.SMEM)
HBM = pl.BlockSpec(memory_space=pltpu.HBM)


def lanes(tile):
    return pl.ds(pl.multiple_of(tile * TILE, TILE), TILE)


def pieces(v):
    first = v.astype(bf16).astype(f32)
    rest = v - first
    second = rest.astype(bf16).astype(f32)
    return first, second, (rest - second).astype(bf16).astype(f32)


def rows_of(shape):
    return lax.broadcasted_iota(jnp.int32, shape, 0)


def streamed_features(x3, depth, radius):
    row = rows_of((8, TILE))
    squares = x3 * x3
    rr = radius * radius
    norm = squares[0:1] + squares[1:2] + squares[2:3] + rr
    cut = pieces(jnp.concatenate([x3, radius, norm, norm, rr, rr], axis=0))
    ones = [jnp.where((row == 5) | (row == 7), 1.0, c) for c in cut]
    streamed = jnp.concatenate([ones[a] for a, _ in GROUPS], axis=0).astype(bf16)
    streamed = jnp.concatenate([streamed, jnp.zeros((80, TILE), bf16)], axis=0)
    moved = jnp.concatenate([depth, depth * x3], axis=0)
    p1, p2, p3 = pieces(jnp.concatenate([moved, moved], axis=0))
    weights = jnp.concatenate(
        [jnp.where(row < 4, p1, p2), jnp.where(row < 4, p3, 0.0)], axis=0
    ).astype(bf16)
    return cut, streamed, weights


def held_features(cut):
    row = rows_of((8, TILE))
    blocks = []
    for a, b in GROUPS:
        own = 1.0 if (a, b) in ((0, 0), (0, 1), (0, 2)) else 0.0
        other = 1.0 if (a, b) in ((0, 0), (1, 0), (2, 0)) else 0.0
        scale_d = jnp.where(row < 3, -2.0, jnp.where(row == 3, 2.0, jnp.where(row == 5, own, 0.0)))
        scale_r = jnp.where(row == 3, 2.0, jnp.where(row == 7, own, 0.0))
        dist = cut[b] * scale_d + jnp.where(row == 4, other, 0.0)
        reach = cut[b] * scale_r + jnp.where(row == 6, other, 0.0)
        blocks.append(jnp.concatenate([dist, reach], axis=1))
    held = jnp.concatenate(blocks, axis=0).astype(bf16)
    return jnp.concatenate([held, jnp.zeros((80, 2 * TILE), bf16)], axis=0)


def store_tiles(a_out, p_out, first, made):
    eye = (rows_of((TILE, TILE)) == lax.broadcasted_iota(jnp.int32, (TILE, TILE), 1)).astype(bf16)
    for n in range(0, len(made), 2):
        pair = jnp.concatenate([made[n][1], made[n + 1][1]], axis=0)
        turned = lax.dot_general(
            eye, pair, (((1,), (1,)), ((), ())), preferred_element_type=f32
        ).astype(bf16)
        for h in range(2):
            a_out[first + n + h] = turned[:, h * TILE : (h + 1) * TILE]
            p_out[first + n + h] = made[n + h][2]


def take(src, idx):
    return jnp.take_along_axis(src, idx, axis=1, mode="promise_in_bounds")


def pair_sums(order, steps, lists, a, b, p, join, own_tiles, tiles_ext):
    def step(n, carry):
        for h in range(UNROLL):
            u = order[n * UNROLL + h]
            m = u // own_tiles
            t = u - m * own_tiles
            held = b[u]
            acc = jnp.zeros((16, 2 * TILE), f32)
            for k in range(PARTNERS):
                q = m * tiles_ext + lists[m, k, t]
                both = jnp.dot(a[q], held, preferred_element_type=f32)
                reach = both[:, TILE:]
                inv = pltpu.reciprocal(both[:, :TILE], approx=True)
                ratio = reach * inv
                cubed = ratio * ratio * ratio
                sixth = cubed * cubed
                energy = sixth - cubed
                coeff = (energy + sixth) * inv
                high = coeff.astype(bf16)
                low = (coeff - high.astype(f32)).astype(bf16)
                left = jnp.concatenate([high, low], axis=0)
                right = jnp.concatenate([energy.astype(bf16), jnp.zeros((TILE, TILE), bf16)], axis=0)
                weights = p[q]
                acc += jnp.dot(
                    jnp.concatenate([weights, weights], axis=1),
                    jnp.concatenate([left, right], axis=1),
                    preferred_element_type=f32,
                )
            joined = acc[0:4] + acc[4:8] + acc[8:12]
            join[u] = jnp.concatenate([joined[:, :TILE], joined[:, TILE:]], axis=0)
        return carry

    lax.fori_loop(0, steps, step, 0)


def prep_kernel(
    coords_in, types_in, well_in, radius_in, lists_in,
    feats, first, last, depth, radius, tables, lists, place,
    types, narrow, sem,
):
    images = feats.shape[1]
    moves = (
        (types_in, types), (well_in, narrow.at[0]), (radius_in, narrow.at[1]),
        (coords_in, feats.at[0:3]), (lists_in, lists),
    )
    copies = [pltpu.make_async_copy(src, dst, sem.at[n]) for n, (src, dst) in enumerate(moves)]
    for copy in copies:
        copy.start()
    slab, image = lax.axis_index("space"), lax.axis_index("image")
    place[0] = (slab > 0).astype(jnp.int32)
    place[1] = (slab < lax.axis_size("space") - 1).astype(jnp.int32)
    place[2] = (image == 0).astype(jnp.int32)
    place[3] = (image == lax.axis_size("image") - 1).astype(jnp.int32)
    for copy in copies[:3]:
        copy.wait()
    for n in range(2):
        tables[n : n + 1] = jnp.concatenate([narrow[n], jnp.zeros_like(narrow[n])], axis=1)
    wells = jnp.broadcast_to(tables[0:1], (8, TILE))
    radii = jnp.broadcast_to(tables[1:2], (8, TILE))
    for n in range(types.shape[0] // 8):
        kind = types[8 * n : 8 * n + 8]
        depth[8 * n : 8 * n + 8] = take(wells, kind)
        radius[8 * n : 8 * n + 8] = take(radii, kind)
        kind = kind.astype(f32)
        for h in range(8):
            t = 8 * n + h
            feats[3, :, t * TILE : (t + 1) * TILE] = jnp.broadcast_to(
                kind[h : h + 1], (images, TILE)
            )
    for copy in copies[3:]:
        copy.wait()
    for c in range(3):
        first[c] = feats[c, 0:1]
        last[c] = feats[c, images - 1 : images]


def own_kernel(
    lists, place, coords, depth_s, radius_s,
    a, b, p, join, center, order, count,
    near,
):
    images = coords.shape[1]
    own_tiles = depth_s.shape[0]
    tiles_ext = a.shape[0] // images
    for c in range(3):
        total = coords[c, :, 0:TILE]
        for t in range(1, own_tiles):
            total = total + coords[c, :, t * TILE : (t + 1) * TILE]
        middle = jnp.sum(total, axis=1, keepdims=True) * (1.0 / (own_tiles * TILE))
        for m in range(images):
            center[m, c : c + 1] = jnp.broadcast_to(middle[m : m + 1], (1, TILE))

    n_near, n_far = jnp.int32(0), jnp.int32(0)
    for m in range(images):
        middle = center[m, 0:3]

        def build(n, carry):
            n_near, n_far = carry
            made = []
            for h in range(8):
                t = 8 * n + h
                u = m * own_tiles + t
                x3 = jnp.concatenate([coords[c, m : m + 1, lanes(t)] for c in range(3)], axis=0)
                made.append(
                    streamed_features(x3 - middle, depth_s[pl.ds(t, 1)], radius_s[pl.ds(t, 1)])
                )
                b[u] = held_features(made[-1][0])
                last = lists[m, 0, t]
                for k in range(1, PARTNERS):
                    last = jnp.maximum(last, lists[m, k, t])
                inside = (last < own_tiles).astype(jnp.int32)
                near[n_near] = u
                order[n_far] = u
                n_near = n_near + inside
                n_far = n_far + (1 - inside)
            store_tiles(a, p, m * tiles_ext + 8 * n, made)
            return n_near, n_far

        n_near, n_far = lax.fori_loop(0, own_tiles // 8, build, (n_near, n_far))
    steps = n_near // UNROLL

    def move(n, n_far):
        order[n_far] = near[n]
        return n_far + 1

    n_far = lax.fori_loop(steps * UNROLL, n_near, move, n_far)
    count[0] = n_far // UNROLL
    pair_sums(near, steps, lists, a, b, p, join, own_tiles, tiles_ext)


def rest_kernel(
    lists, place, order, count, coords, below, above, own_depth, tables, hidx, ref, restr, prev, nxt,
    center, b, a_in, p_in, join_in,
    force, sums, a, p, join,
    halo_x, depth_s, radius_s,
):
    images = coords.shape[1]
    own_tiles = own_depth.shape[0]
    tiles_ext = a.shape[0] // images
    halo_tiles = tiles_ext - own_tiles
    side_tiles = halo_tiles // 2
    wells = jnp.broadcast_to(tables[0:1], (8, TILE))
    radii = jnp.broadcast_to(tables[1:2], (8, TILE))

    for side, source in enumerate((below, above)):
        low, high = [], []
        for m in range(images):
            idx = jnp.concatenate(
                [hidx[m, side : side + 1, q * TILE : (q + 1) * TILE] for q in range(side_tiles)],
                axis=0,
            )
            low.append(idx & (TILE - 1))
            high.append(idx >> 7)

        def gather_row(r, carry):
            out = []
            for m in range(images):
                hit = high[m] == r
                for c in range(4):
                    wide = jnp.broadcast_to(source[c, m : m + 1, lanes(r)], (8, TILE))
                    out.append(jnp.where(hit, take(wide, low[m]), carry[4 * m + c]))
            return tuple(out)

        zero = jnp.zeros((8, TILE), f32)
        found = lax.fori_loop(0, own_tiles, gather_row, (zero,) * (4 * images), unroll=8)
        inside = place[side].astype(f32)
        spot = slice(side * side_tiles, (side + 1) * side_tiles)
        for m in range(images):
            for c in range(3):
                halo_x[m, c, spot] = found[4 * m + c]
            kind = found[4 * m + 3].astype(jnp.int32)
            depth_s[m, spot] = take(wells, kind) * inside
            radius_s[m, spot] = take(radii, kind)

    for m in range(images):
        middle = center[m, 0:3]

        def build(n, carry):
            made = []
            for h in range(8):
                t = 8 * n + h
                x3 = jnp.concatenate([halo_x[m, c, pl.ds(t, 1)] for c in range(3)], axis=0)
                made.append(
                    streamed_features(
                        x3 - middle, depth_s[m, pl.ds(t, 1)], radius_s[m, pl.ds(t, 1)]
                    )
                )
            store_tiles(a, p, m * tiles_ext + own_tiles + 8 * n, made)
            return carry

        lax.fori_loop(0, halo_tiles // 8, build, 0)

    pair_sums(order, count[0], lists, a, b, p, join, own_tiles, tiles_ext)

    def finish(n, carry):
        carry = list(carry)
        for h in range(4):
            t = 4 * n + h
            at = lanes(t)
            depth = own_depth[pl.ds(t, 1)]
            stiff = restr[:, at]
            rows = [join[m * own_tiles + t] for m in range(images)]
            weight = jnp.concatenate([r[0:1] for r in rows], axis=0)
            carry[5] += 2.0 * depth * jnp.concatenate([r[4:5] for r in rows], axis=0)
            for c in range(3):
                x = coords[c, :, at]
                middle = jnp.concatenate([center[m, c : c + 1] for m in range(images)], axis=0)
                moved = jnp.concatenate([r[1 + c : 2 + c] for r in rows], axis=0)
                offset = x - ref[c : c + 1, at]
                pull = stiff * offset
                total = 24.0 * depth * ((x - middle) * weight - moved) - pull
                force[c, :, at] = total
                before = jnp.concatenate([prev[c, :, at], x[0:1]], axis=0)
                after = jnp.concatenate([x[1:2], nxt[c, :, at]], axis=0)
                ahead, behind = after - x, x - before
                both_ways, bend = ahead + behind, ahead - behind
                carry[0] += both_ways * both_ways
                carry[1] += both_ways * bend
                carry[2] += bend * bend
                carry[3] += total * both_ways
                carry[4] += total * bend
                carry[5] += 0.5 * pull * offset
        return tuple(carry)

    zero = jnp.zeros((images, TILE), f32)
    line = lax.fori_loop(0, own_tiles // 4, finish, (zero,) * 6)
    line = jnp.concatenate(list(line) + [jnp.zeros((16 - 6 * images, TILE), f32)], axis=0)
    row, lane = rows_of((16, 16)), lax.broadcasted_iota(jnp.int32, (16, 16), 1)
    totals = jnp.sum(line, axis=1, keepdims=True)
    totals = jnp.sum(jnp.where(row == lane, totals, 0.0), axis=0, keepdims=True)
    sums[...] = jnp.broadcast_to(totals, (16, 16))


def band_kernel(place, shares, force, coords, prev, nxt, out, energies):
    total = jnp.sum(shares[...], axis=0, keepdims=True)
    images, atoms = coords.shape[1], coords.shape[2]
    parts = []
    for m in range(images):
        s_sq, cross, b_sq, f_s, f_b, energy = [
            total[:, images * n + m : images * n + m + 1] for n in range(6)
        ]
        energies[m] = (energy / (16 * atoms))[0, 0]
        base = 0.25 * (s_sq + b_sq) + small_eps
        ahead_sq, behind_sq = base + 0.5 * cross, base - 0.5 * cross
        ahead_len, behind_len = jnp.sqrt(ahead_sq), jnp.sqrt(behind_sq)
        inverse_sum = 1.0 / ahead_len + 1.0 / behind_len
        alpha = 0.5 * inverse_sum
        beta = -0.5 * cross / (ahead_sq * behind_sq * inverse_sum)
        tan_sq = alpha * alpha * s_sq + 2.0 * alpha * beta * cross + beta * beta * b_sq
        tan_len = jnp.sqrt(jnp.maximum(tan_sq, 0.0) + small_eps)
        along = (alpha * f_s + beta * f_b) / tan_len
        stretch = cross / (ahead_len + behind_len)
        gain = (spring_k * stretch - along) / tan_len
        gain = jnp.where(place[2 + m] == 1, 0.0, gain)
        parts.append((gain * alpha, gain * beta))
    for_s = jnp.concatenate([jnp.broadcast_to(q[0], (1, TILE)) for q in parts], axis=0)
    for_b = jnp.concatenate([jnp.broadcast_to(q[1], (1, TILE)) for q in parts], axis=0)
    for t in range(atoms // TILE):
        at = slice(t * TILE, (t + 1) * TILE)
        for c in range(3):
            x = coords[c, :, at]
            before = jnp.concatenate([prev[c, :, at], x[0:1]], axis=0)
            after = jnp.concatenate([x[1:2], nxt[c, :, at]], axis=0)
            ahead, behind = after - x, x - before
            out[c, :, at] = force[c, :, at] + for_s * (ahead + behind) + for_b * (ahead - behind)


def ring(axis, step):
    n = lax.axis_size(axis)
    return [(i, (i + step) % n) for i in range(n)]


def shape(dims, dtype=f32):
    return jax.ShapeDtypeStruct(dims, dtype)


def params(mib, **more):
    return dict(compiler_params=pltpu.CompilerParams(vmem_limit_bytes=mib << 20), **more)


def body(
    coords, ref_coords, restraint, atom_types, well_table, radius_table, tile_lists, halo_index
):
    images, _, atoms = coords.shape
    tiles = atoms // TILE
    tiles_ext = tiles + 2 * halo_index.shape[2] // TILE
    kinds = well_table.shape[0]
    feats, first, last, depth, radius, tables, lists, place = pl.pallas_call(
        prep_kernel,
        out_shape=(
            shape((4, images, atoms)),
            shape((3, 1, atoms)),
            shape((3, 1, atoms)),
            shape((tiles, TILE)),
            shape((tiles, TILE)),
            shape((2, TILE)),
            shape(tile_lists.shape, jnp.int32),
            shape((4,), jnp.int32),
        ),
        in_specs=[HBM] * 5,
        out_specs=(VMEM,) * 7 + (SMEM,),
        scratch_shapes=[
            pltpu.VMEM((tiles, TILE), jnp.int32),
            pltpu.VMEM((2, 1, kinds), f32),
            pltpu.SemaphoreType.DMA((5,)),
        ],
        name="prep",
        **params(8),
    )(
        coords.transpose(1, 0, 2), atom_types.reshape(tiles, TILE), well_table[None],
        radius_table[None], tile_lists,
    )
    below = lax.ppermute(feats, "space", ring("space", 1))
    above = lax.ppermute(feats, "space", ring("space", -1))
    prev = lax.ppermute(last, "image", ring("image", 1))
    nxt = lax.ppermute(first, "image", ring("image", -1))
    own = images * tiles
    a, b, p, join, center, order, count = pl.pallas_call(
        own_kernel,
        out_shape=(
            shape((images * tiles_ext, TILE, TILE), bf16),
            shape((own, TILE, 2 * TILE), bf16),
            shape((images * tiles_ext, 16, TILE), bf16),
            shape((own, 8, TILE)),
            shape((images, 8, TILE)),
            shape((own,), jnp.int32),
            shape((1,), jnp.int32),
        ),
        in_specs=[SMEM] * 2 + [VMEM] * 3,
        out_specs=(VMEM,) * 5 + (SMEM,) * 2,
        scratch_shapes=[
            pltpu.SMEM((own,), jnp.int32),
        ],
        cost_estimate=pl.CostEstimate(flops=60 * 10**9, bytes_accessed=10**6, transcendentals=0),
        name="own",
        **params(16),
    )(lists, place, feats, depth, radius)
    force, sums, *_ = pl.pallas_call(
        rest_kernel,
        out_shape=(
            shape((3, images, atoms)),
            shape((16, 16)),
            shape(a.shape, bf16),
            shape(p.shape, bf16),
            shape(join.shape),
        ),
        in_specs=[SMEM] * 4 + [VMEM] * 15,
        out_specs=(VMEM,) * 5,
        input_output_aliases={16: 2, 17: 3, 18: 4},
        scratch_shapes=[
            pltpu.VMEM((images, 3, tiles_ext - tiles, TILE), f32),
            pltpu.VMEM((images, tiles_ext - tiles, TILE), f32),
            pltpu.VMEM((images, tiles_ext - tiles, TILE), f32),
        ],
        name="rest",
        **params(16),
    )(
        lists, place, order, count, feats, below, above, depth, tables, halo_index,
        ref_coords, restraint[None], prev, nxt, center, b, a, p, join,
    )
    shares = lax.all_to_all(sums, "space", 0, 0, tiled=True)
    out, energies = pl.pallas_call(
        band_kernel,
        out_shape=(shape((3, images, atoms)), shape((images,))),
        in_specs=[SMEM] + [VMEM] * 5,
        out_specs=(VMEM, SMEM),
        name="band",
        **params(8),
    )(place, shares, force, feats, prev, nxt)
    return out.transpose(1, 0, 2), energies


def solution(mesh):
    in_specs = (
        P("image", None, "space"),
        P(None, "space"),
        P("space"),
        P("space"),
        P(),
        P(),
        P("image", None, "space"),
        P("image", None, "space"),
    )
    out_specs = (P("image", None, "space"), P("image"))
    return jax.shard_map(body, mesh=mesh, in_specs=in_specs, out_specs=out_specs, check_vma=False)
```

```python
import jax
import jax.numpy as jnp
from jax import lax
from jax.experimental import pallas as pl
from jax.experimental.pallas import tpu as pltpu
from jax.sharding import PartitionSpec as P

TILE = 128
PARTNERS = 4
UNROLL = 32
BUILD = 16
spring_k = 2.0
small_eps = 1e-06
f32, bf16 = jnp.float32, jnp.bfloat16
GROUPS = ((0, 0), (0, 1), (1, 0), (0, 2), (2, 0), (1, 1))
VMEM = pl.BlockSpec(memory_space=pltpu.VMEM)
SMEM = pl.BlockSpec(memory_space=pltpu.SMEM)


def lanes(tile):
    return pl.ds(pl.multiple_of(tile * TILE, TILE), TILE)


def pieces(v):
    first = v.astype(bf16).astype(f32)
    rest = v - first
    second = rest.astype(bf16).astype(f32)
    return first, second, (rest - second).astype(bf16).astype(f32)


def rows_of(shape):
    return lax.broadcasted_iota(jnp.int32, shape, 0)


def streamed_features(x3, depth, radius):
    row = rows_of((8, TILE))
    squares = x3 * x3
    rr = radius * radius
    norm = squares[0:1] + squares[1:2] + squares[2:3] + rr
    cut = pieces(jnp.concatenate([x3, radius, norm, norm, rr, rr], axis=0))
    ones = [jnp.where((row == 5) | (row == 7), 1.0, c) for c in cut]
    streamed = jnp.concatenate([ones[a] for a, _ in GROUPS], axis=0).astype(bf16)
    streamed = jnp.concatenate([streamed, jnp.zeros((80, TILE), bf16)], axis=0)
    moved = jnp.concatenate([depth, depth * x3], axis=0)
    p1, p2, p3 = pieces(jnp.concatenate([moved, moved], axis=0))
    weights = jnp.concatenate(
        [jnp.where(row < 4, p1, p2), jnp.where(row < 4, p3, 0.0)], axis=0
    ).astype(bf16)
    return cut, streamed, weights


def held_features(cut):
    row = rows_of((8, TILE))
    blocks = []
    for a, b in GROUPS:
        own = 1.0 if (a, b) in ((0, 0), (0, 1), (0, 2)) else 0.0
        other = 1.0 if (a, b) in ((0, 0), (1, 0), (2, 0)) else 0.0
        scale_d = jnp.where(row < 3, -2.0, jnp.where(row == 3, 2.0, jnp.where(row == 5, own, 0.0)))
        scale_r = jnp.where(row == 3, 2.0, jnp.where(row == 7, own, 0.0))
        dist = cut[b] * scale_d + jnp.where(row == 4, other, 0.0)
        reach = cut[b] * scale_r + jnp.where(row == 6, other, 0.0)
        blocks.append(jnp.concatenate([dist, reach], axis=1))
    held = jnp.concatenate(blocks, axis=0).astype(bf16)
    return jnp.concatenate([held, jnp.zeros((80, 2 * TILE), bf16)], axis=0)


def store_tiles(a_out, p_out, first, made):
    eye = (rows_of((TILE, TILE)) == lax.broadcasted_iota(jnp.int32, (TILE, TILE), 1)).astype(bf16)
    for n in range(0, len(made), 2):
        pair = jnp.concatenate([made[n][1], made[n + 1][1]], axis=0)
        turned = lax.dot_general(
            eye, pair, (((1,), (1,)), ((), ())), preferred_element_type=f32
        ).astype(bf16)
        for h in range(2):
            a_out[first + n + h] = turned[:, h * TILE : (h + 1) * TILE]
            p_out[first + n + h] = made[n + h][2]


def take(src, idx):
    return jnp.take_along_axis(src, idx, axis=1, mode="promise_in_bounds")


def pair_sums(order, steps, lists, a, b, p, join, own_tiles, tiles_ext):
    def step(n, carry):
        for h in range(UNROLL):
            u = order[n * UNROLL + h]
            m = u // own_tiles
            t = u - m * own_tiles
            held = b[u]
            acc = jnp.zeros((16, 2 * TILE), f32)
            for k in range(PARTNERS):
                q = m * tiles_ext + lists[m, k, t]
                both = jnp.dot(a[q], held, preferred_element_type=f32)
                reach = both[:, TILE:]
                inv = pltpu.reciprocal(both[:, :TILE], approx=True)
                ratio = reach * inv
                cubed = ratio * ratio * ratio
                sixth = cubed * cubed
                energy = sixth - cubed
                coeff = (energy + sixth) * inv
                high = coeff.astype(bf16)
                low = (coeff - high.astype(f32)).astype(bf16)
                left = jnp.concatenate([high, low], axis=0)
                right = jnp.concatenate([energy.astype(bf16), jnp.zeros((TILE, TILE), bf16)], axis=0)
                weights = p[q]
                acc += jnp.dot(
                    jnp.concatenate([weights, weights], axis=1),
                    jnp.concatenate([left, right], axis=1),
                    preferred_element_type=f32,
                )
            joined = acc[0:4] + acc[4:8] + acc[8:12]
            join[u] = jnp.concatenate([joined[:, :TILE], joined[:, TILE:]], axis=0)
        return carry

    lax.fori_loop(0, steps, step, 0)


def table(values):
    wide = jnp.concatenate([values[...], jnp.zeros_like(values[...])], axis=1)
    return jnp.broadcast_to(wide, (8, TILE))


def prep_kernel(coords_in, types, feats, first, last, place):
    images = feats.shape[1]
    slab, image = lax.axis_index("space"), lax.axis_index("image")
    place[0] = (slab > 0).astype(jnp.int32)
    place[1] = (slab < lax.axis_size("space") - 1).astype(jnp.int32)
    place[2] = (image == 0).astype(jnp.int32)
    place[3] = (image == lax.axis_size("image") - 1).astype(jnp.int32)
    for n in range(types.shape[0] // 8):
        kind = types[8 * n : 8 * n + 8].astype(f32)
        for h in range(8):
            t = 8 * n + h
            feats[3, :, t * TILE : (t + 1) * TILE] = jnp.broadcast_to(
                kind[h : h + 1], (images, TILE)
            )
    for c in range(3):
        rows = coords_in[c]
        feats[c] = rows
        first[c] = rows[0:1]
        last[c] = rows[images - 1 : images]


def own_kernel(
    lists, place, coords, types, well, radius,
    a, b, p, join, center, depth_s, order, count,
    near, radius_s,
):
    images = coords.shape[1]
    own_tiles = types.shape[0]
    tiles_ext = a.shape[0] // images
    wells, radii = table(well), table(radius)
    for n in range(own_tiles // 8):
        kind = types[8 * n : 8 * n + 8]
        depth_s[8 * n : 8 * n + 8] = take(wells, kind)
        radius_s[8 * n : 8 * n + 8] = take(radii, kind)
    for c in range(3):
        total = coords[c, :, 0:TILE]
        for t in range(1, own_tiles):
            total = total + coords[c, :, t * TILE : (t + 1) * TILE]
        middle = jnp.sum(total, axis=1, keepdims=True) * (1.0 / (own_tiles * TILE))
        for m in range(images):
            center[m, c : c + 1] = jnp.broadcast_to(middle[m : m + 1], (1, TILE))

    n_near, n_far = jnp.int32(0), jnp.int32(0)
    for m in range(images):
        middle = center[m, 0:3]

        def build(n, carry):
            n_near, n_far = carry
            made = []
            for h in range(BUILD):
                t = BUILD * n + h
                u = m * own_tiles + t
                x3 = jnp.concatenate([coords[c, m : m + 1, lanes(t)] for c in range(3)], axis=0)
                made.append(
                    streamed_features(x3 - middle, depth_s[pl.ds(t, 1)], radius_s[pl.ds(t, 1)])
                )
                b[u] = held_features(made[-1][0])
                last = lists[m, 0, t]
                for k in range(1, PARTNERS):
                    last = jnp.maximum(last, lists[m, k, t])
                inside = (last < own_tiles).astype(jnp.int32)
                near[n_near] = u
                order[n_far] = u
                n_near = n_near + inside
                n_far = n_far + (1 - inside)
            store_tiles(a, p, m * tiles_ext + BUILD * n, made)
            return n_near, n_far

        n_near, n_far = lax.fori_loop(0, own_tiles // BUILD, build, (n_near, n_far))
    steps = n_near // UNROLL

    def move(n, n_far):
        order[n_far] = near[n]
        return n_far + 1

    n_far = lax.fori_loop(steps * UNROLL, n_near, move, n_far)
    count[0] = n_far // UNROLL
    pair_sums(near, steps, lists, a, b, p, join, own_tiles, tiles_ext)


def rest_kernel(
    lists, place, order, count, coords, below, above, own_depth, well, radius, hidx, ref, restr, prev, nxt,
    center, b, a_in, p_in, join_in,
    force, sums, a, p, join,
    halo_x, depth_s, radius_s,
):
    images = coords.shape[1]
    own_tiles = own_depth.shape[0]
    tiles_ext = a.shape[0] // images
    halo_tiles = tiles_ext - own_tiles
    side_tiles = halo_tiles // 2
    wells, radii = table(well), table(radius)

    for side, source in enumerate((below, above)):
        low, high = [], []
        for m in range(images):
            idx = jnp.concatenate(
                [hidx[m, side : side + 1, q * TILE : (q + 1) * TILE] for q in range(side_tiles)],
                axis=0,
            )
            low.append(idx & (TILE - 1))
            high.append(idx >> 7)

        def gather_row(r, carry):
            out = []
            for m in range(images):
                hit = high[m] == r
                for c in range(4):
                    wide = jnp.broadcast_to(source[c, m : m + 1, lanes(r)], (8, TILE))
                    out.append(jnp.where(hit, take(wide, low[m]), carry[4 * m + c]))
            return tuple(out)

        zero = jnp.zeros((8, TILE), f32)
        found = lax.fori_loop(0, own_tiles, gather_row, (zero,) * (4 * images), unroll=8)
        inside = place[side].astype(f32)
        spot = slice(side * side_tiles, (side + 1) * side_tiles)
        for m in range(images):
            for c in range(3):
                halo_x[m, c, spot] = found[4 * m + c]
            kind = found[4 * m + 3].astype(jnp.int32)
            depth_s[m, spot] = take(wells, kind) * inside
            radius_s[m, spot] = take(radii, kind)

    for m in range(images):
        middle = center[m, 0:3]

        def build(n, carry):
            made = []
            for h in range(BUILD):
                t = BUILD * n + h
                x3 = jnp.concatenate([halo_x[m, c, pl.ds(t, 1)] for c in range(3)], axis=0)
                made.append(
                    streamed_features(
                        x3 - middle, depth_s[m, pl.ds(t, 1)], radius_s[m, pl.ds(t, 1)]
                    )
                )
            store_tiles(a, p, m * tiles_ext + own_tiles + BUILD * n, made)
            return carry

        lax.fori_loop(0, halo_tiles // BUILD, build, 0)

    pair_sums(order, count[0], lists, a, b, p, join, own_tiles, tiles_ext)

    def finish(n, carry):
        carry = list(carry)
        for h in range(4):
            t = 4 * n + h
            at = lanes(t)
            depth = own_depth[pl.ds(t, 1)]
            stiff = restr[:, at]
            rows = [join[m * own_tiles + t] for m in range(images)]
            weight = jnp.concatenate([r[0:1] for r in rows], axis=0)
            carry[5] += 2.0 * depth * jnp.concatenate([r[4:5] for r in rows], axis=0)
            for c in range(3):
                x = coords[c, :, at]
                middle = jnp.concatenate([center[m, c : c + 1] for m in range(images)], axis=0)
                moved = jnp.concatenate([r[1 + c : 2 + c] for r in rows], axis=0)
                offset = x - ref[c : c + 1, at]
                pull = stiff * offset
                total = 24.0 * depth * ((x - middle) * weight - moved) - pull
                force[c, :, at] = total
                before = jnp.concatenate([prev[c, :, at], x[0:1]], axis=0)
                after = jnp.concatenate([x[1:2], nxt[c, :, at]], axis=0)
                ahead, behind = after - x, x - before
                both_ways, bend = ahead + behind, ahead - behind
                carry[0] += both_ways * both_ways
                carry[1] += both_ways * bend
                carry[2] += bend * bend
                carry[3] += total * both_ways
                carry[4] += total * bend
                carry[5] += 0.5 * pull * offset
        return tuple(carry)

    zero = jnp.zeros((images, TILE), f32)
    line = lax.fori_loop(0, own_tiles // 4, finish, (zero,) * 6)
    line = jnp.concatenate(list(line) + [jnp.zeros((16 - 6 * images, TILE), f32)], axis=0)
    row, lane = rows_of((16, 16)), lax.broadcasted_iota(jnp.int32, (16, 16), 1)
    totals = jnp.sum(line, axis=1, keepdims=True)
    totals = jnp.sum(jnp.where(row == lane, totals, 0.0), axis=0, keepdims=True)
    sums[...] = jnp.broadcast_to(totals, (16, 16))


def band_kernel(place, shares, force, coords, prev, nxt, out, energies):
    total = jnp.sum(shares[...], axis=0, keepdims=True)
    images, atoms = coords.shape[1], coords.shape[2]
    parts = []
    for m in range(images):
        s_sq, cross, b_sq, f_s, f_b, energy = [
            total[:, images * n + m : images * n + m + 1] for n in range(6)
        ]
        energies[m] = (energy / (16 * atoms))[0, 0]
        base = 0.25 * (s_sq + b_sq) + small_eps
        ahead_sq, behind_sq = base + 0.5 * cross, base - 0.5 * cross
        ahead_len, behind_len = jnp.sqrt(ahead_sq), jnp.sqrt(behind_sq)
        inverse_sum = 1.0 / ahead_len + 1.0 / behind_len
        alpha = 0.5 * inverse_sum
        beta = -0.5 * cross / (ahead_sq * behind_sq * inverse_sum)
        tan_sq = alpha * alpha * s_sq + 2.0 * alpha * beta * cross + beta * beta * b_sq
        tan_len = jnp.sqrt(jnp.maximum(tan_sq, 0.0) + small_eps)
        along = (alpha * f_s + beta * f_b) / tan_len
        stretch = cross / (ahead_len + behind_len)
        gain = (spring_k * stretch - along) / tan_len
        gain = jnp.where(place[2 + m] == 1, 0.0, gain)
        parts.append((gain * alpha, gain * beta))
    for_s = jnp.concatenate([jnp.broadcast_to(q[0], (1, TILE)) for q in parts], axis=0)
    for_b = jnp.concatenate([jnp.broadcast_to(q[1], (1, TILE)) for q in parts], axis=0)
    for t in range(atoms // TILE):
        at = slice(t * TILE, (t + 1) * TILE)
        for c in range(3):
            x = coords[c, :, at]
            before = jnp.concatenate([prev[c, :, at], x[0:1]], axis=0)
            after = jnp.concatenate([x[1:2], nxt[c, :, at]], axis=0)
            ahead, behind = after - x, x - before
            out[c, :, at] = force[c, :, at] + for_s * (ahead + behind) + for_b * (ahead - behind)


def ring(axis, step):
    n = lax.axis_size(axis)
    return [(i, (i + step) % n) for i in range(n)]


def shape(dims, dtype=f32):
    return jax.ShapeDtypeStruct(dims, dtype)


def params(mib, **more):
    return dict(compiler_params=pltpu.CompilerParams(vmem_limit_bytes=mib << 20), **more)


def body(
    coords, ref_coords, restraint, atom_types, well_table, radius_table, tile_lists, halo_index
):
    images, _, atoms = coords.shape
    tiles = atoms // TILE
    tiles_ext = tiles + 2 * halo_index.shape[2] // TILE
    types = atom_types.reshape(tiles, TILE)
    well, radius = well_table[None], radius_table[None]
    feats, first, last, place = pl.pallas_call(
        prep_kernel,
        out_shape=(
            shape((4, images, atoms)),
            shape((3, 1, atoms)),
            shape((3, 1, atoms)),
            shape((4,), jnp.int32),
        ),
        in_specs=[VMEM] * 2,
        out_specs=(VMEM,) * 3 + (SMEM,),
        cost_estimate=pl.CostEstimate(flops=10**10, bytes_accessed=10**6, transcendentals=0),
        name="prep",
        **params(8),
    )(coords.transpose(1, 0, 2), types)
    below = lax.ppermute(feats, "space", ring("space", 1))
    above = lax.ppermute(feats, "space", ring("space", -1))
    prev = lax.ppermute(last, "image", ring("image", 1))
    nxt = lax.ppermute(first, "image", ring("image", -1))
    own = images * tiles
    a, b, p, join, center, depth, order, count = pl.pallas_call(
        own_kernel,
        out_shape=(
            shape((images * tiles_ext, TILE, TILE), bf16),
            shape((own, TILE, 2 * TILE), bf16),
            shape((images * tiles_ext, 16, TILE), bf16),
            shape((own, 8, TILE)),
            shape((images, 8, TILE)),
            shape((tiles, TILE)),
            shape((own,), jnp.int32),
            shape((1,), jnp.int32),
        ),
        in_specs=[SMEM] * 2 + [VMEM] * 4,
        out_specs=(VMEM,) * 6 + (SMEM,) * 2,
        scratch_shapes=[
            pltpu.SMEM((own,), jnp.int32),
            pltpu.VMEM((tiles, TILE), f32),
        ],
        cost_estimate=pl.CostEstimate(flops=60 * 10**9, bytes_accessed=10**6, transcendentals=0),
        name="own",
        **params(16),
    )(tile_lists, place, feats, types, well, radius)
    force, sums, *_ = pl.pallas_call(
        rest_kernel,
        out_shape=(
            shape((3, images, atoms)),
            shape((16, 16)),
            shape(a.shape, bf16),
            shape(p.shape, bf16),
            shape(join.shape),
        ),
        in_specs=[SMEM] * 4 + [VMEM] * 16,
        out_specs=(VMEM,) * 5,
        input_output_aliases={17: 2, 18: 3, 19: 4},
        scratch_shapes=[
            pltpu.VMEM((images, 3, tiles_ext - tiles, TILE), f32),
            pltpu.VMEM((images, tiles_ext - tiles, TILE), f32),
            pltpu.VMEM((images, tiles_ext - tiles, TILE), f32),
        ],
        name="rest",
        **params(16),
    )(
        tile_lists, place, order, count, feats, below, above, depth, well, radius, halo_index,
        ref_coords, restraint[None], prev, nxt, center, b, a, p, join,
    )
    shares = lax.all_to_all(sums, "space", 0, 0, tiled=True)
    out, energies = pl.pallas_call(
        band_kernel,
        out_shape=(shape((3, images, atoms)), shape((images,))),
        in_specs=[SMEM] + [VMEM] * 5,
        out_specs=(VMEM, SMEM),
        name="band",
        **params(8),
    )(place, shares, force, feats, prev, nxt)
    return out.transpose(1, 0, 2), energies


def solution(mesh):
    in_specs = (
        P("image", None, "space"),
        P(None, "space"),
        P("space"),
        P("space"),
        P(),
        P(),
        P("image", None, "space"),
        P("image", None, "space"),
    )
    out_specs = (P("image", None, "space"), P("image"))
    return jax.shard_map(body, mesh=mesh, in_specs=in_specs, out_specs=out_specs, check_vma=False)
```

```python
import jax
import jax.numpy as jnp
from jax import lax
from jax.experimental import pallas as pl
from jax.experimental.pallas import tpu as pltpu
from jax.sharding import PartitionSpec as P

TILE = 128
PARTNERS = 4
UNROLL = 32
BUILD = 16
spring_k = 2.0
small_eps = 1e-06
f32, bf16 = jnp.float32, jnp.bfloat16
GROUPS = ((0, 0), (0, 1), (1, 0), (0, 2), (2, 0), (1, 1))
VMEM = pl.BlockSpec(memory_space=pltpu.VMEM)
SMEM = pl.BlockSpec(memory_space=pltpu.SMEM)


def lanes(tile):
    return pl.ds(pl.multiple_of(tile * TILE, TILE), TILE)


def pieces(v):
    first = v.astype(bf16).astype(f32)
    rest = v - first
    second = rest.astype(bf16).astype(f32)
    return first, second, (rest - second).astype(bf16).astype(f32)


def rows_of(shape):
    return lax.broadcasted_iota(jnp.int32, shape, 0)


def streamed_features(x3, depth, radius):
    row = rows_of((8, TILE))
    squares = x3 * x3
    rr = radius * radius
    norm = squares[0:1] + squares[1:2] + squares[2:3] + rr
    cut = pieces(jnp.concatenate([x3, radius, norm, norm, rr, rr], axis=0))
    ones = [jnp.where((row == 5) | (row == 7), 1.0, c) for c in cut]
    streamed = jnp.concatenate([ones[a] for a, _ in GROUPS], axis=0).astype(bf16)
    streamed = jnp.concatenate([streamed, jnp.zeros((80, TILE), bf16)], axis=0)
    moved = jnp.concatenate([depth, depth * x3], axis=0)
    p1, p2, p3 = pieces(jnp.concatenate([moved, moved], axis=0))
    weights = jnp.concatenate(
        [jnp.where(row < 4, p1, p2), jnp.where(row < 4, p3, 0.0)], axis=0
    ).astype(bf16)
    return cut, streamed, weights


def held_features(cut):
    row = rows_of((8, TILE))
    blocks = []
    for a, b in GROUPS:
        own = 1.0 if (a, b) in ((0, 0), (0, 1), (0, 2)) else 0.0
        other = 1.0 if (a, b) in ((0, 0), (1, 0), (2, 0)) else 0.0
        scale_d = jnp.where(row < 3, -2.0, jnp.where(row == 3, 2.0, jnp.where(row == 5, own, 0.0)))
        scale_r = jnp.where(row == 3, 2.0, jnp.where(row == 7, own, 0.0))
        dist = cut[b] * scale_d + jnp.where(row == 4, other, 0.0)
        reach = cut[b] * scale_r + jnp.where(row == 6, other, 0.0)
        blocks.append(jnp.concatenate([dist, reach], axis=1))
    held = jnp.concatenate(blocks, axis=0).astype(bf16)
    return jnp.concatenate([held, jnp.zeros((80, 2 * TILE), bf16)], axis=0)


def store_tiles(a_out, p_out, first, made):
    eye = (rows_of((TILE, TILE)) == lax.broadcasted_iota(jnp.int32, (TILE, TILE), 1)).astype(bf16)
    for n in range(0, len(made), 2):
        pair = jnp.concatenate([made[n][1], made[n + 1][1]], axis=0)
        turned = lax.dot_general(
            eye, pair, (((1,), (1,)), ((), ())), preferred_element_type=f32
        ).astype(bf16)
        for h in range(2):
            a_out[first + n + h] = turned[:, h * TILE : (h + 1) * TILE]
            p_out[first + n + h] = made[n + h][2]


def take(src, idx):
    return jnp.take_along_axis(src, idx, axis=1, mode="promise_in_bounds")


def pair_sums(order, steps, lists, a, b, p, join, own_tiles, tiles_ext):
    def step(n, carry):
        for h in range(UNROLL):
            u = order[n * UNROLL + h]
            m = u // own_tiles
            t = u - m * own_tiles
            held = b[u]
            acc = jnp.zeros((16, 2 * TILE), f32)
            for k in range(PARTNERS):
                q = m * tiles_ext + lists[m, k, t]
                both = jnp.dot(a[q], held, preferred_element_type=f32)
                reach = both[:, TILE:]
                inv = pltpu.reciprocal(both[:, :TILE], approx=True)
                ratio = reach * inv
                cubed = ratio * ratio * ratio
                sixth = cubed * cubed
                energy = sixth - cubed
                coeff = (energy + sixth) * inv
                high = coeff.astype(bf16)
                low = (coeff - high.astype(f32)).astype(bf16)
                left = jnp.concatenate([high, low], axis=0)
                right = jnp.concatenate([energy.astype(bf16), jnp.zeros((TILE, TILE), bf16)], axis=0)
                weights = p[q]
                acc += jnp.dot(
                    jnp.concatenate([weights, weights], axis=1),
                    jnp.concatenate([left, right], axis=1),
                    preferred_element_type=f32,
                )
            joined = acc[0:4] + acc[4:8] + acc[8:12]
            join[u] = jnp.concatenate([joined[:, :TILE], joined[:, TILE:]], axis=0)
        return carry

    lax.fori_loop(0, steps, step, 0)


def table(values):
    wide = jnp.concatenate([values[...], jnp.zeros_like(values[...])], axis=1)
    return jnp.broadcast_to(wide, (8, TILE))


def prep_kernel(coords_in, types, feats, first, last, place):
    images = feats.shape[1]
    slab, image = lax.axis_index("space"), lax.axis_index("image")
    place[0] = (slab > 0).astype(jnp.int32)
    place[1] = (slab < lax.axis_size("space") - 1).astype(jnp.int32)
    place[2] = (image == 0).astype(jnp.int32)
    place[3] = (image == lax.axis_size("image") - 1).astype(jnp.int32)
    for n in range(types.shape[0] // 8):
        kind = types[8 * n : 8 * n + 8].astype(f32)
        for h in range(8):
            t = 8 * n + h
            feats[3, :, t * TILE : (t + 1) * TILE] = jnp.broadcast_to(
                kind[h : h + 1], (images, TILE)
            )
    for c in range(3):
        rows = coords_in[c]
        feats[c] = rows
        first[c] = rows[0:1]
        last[c] = rows[images - 1 : images]


def own_kernel(
    lists, place, coords, types, well, radius,
    a, b, p, join, center, depth_s, order, count,
    near, radius_s,
):
    images = coords.shape[1]
    own_tiles = types.shape[0]
    tiles_ext = a.shape[0] // images
    wells, radii = table(well), table(radius)
    for n in range(own_tiles // 8):
        kind = types[8 * n : 8 * n + 8]
        depth_s[8 * n : 8 * n + 8] = take(wells, kind)
        radius_s[8 * n : 8 * n + 8] = take(radii, kind)
    for c in range(3):
        total = coords[c, :, 0:TILE]
        for t in range(1, own_tiles):
            total = total + coords[c, :, t * TILE : (t + 1) * TILE]
        middle = jnp.sum(total, axis=1, keepdims=True) * (1.0 / (own_tiles * TILE))
        for m in range(images):
            center[m, c : c + 1] = jnp.broadcast_to(middle[m : m + 1], (1, TILE))

    n_near, n_far = jnp.int32(0), jnp.int32(0)
    for m in range(images):
        middle = center[m, 0:3]

        def build(n, carry):
            n_near, n_far = carry
            made = []
            for h in range(BUILD):
                t = BUILD * n + h
                u = m * own_tiles + t
                x3 = jnp.concatenate([coords[c, m : m + 1, lanes(t)] for c in range(3)], axis=0)
                made.append(
                    streamed_features(x3 - middle, depth_s[pl.ds(t, 1)], radius_s[pl.ds(t, 1)])
                )
                b[u] = held_features(made[-1][0])
                last = lists[m, 0, t]
                for k in range(1, PARTNERS):
                    last = jnp.maximum(last, lists[m, k, t])
                inside = (last < own_tiles).astype(jnp.int32)
                near[n_near] = u
                order[n_far] = u
                n_near = n_near + inside
                n_far = n_far + (1 - inside)
            store_tiles(a, p, m * tiles_ext + BUILD * n, made)
            return n_near, n_far

        n_near, n_far = lax.fori_loop(0, own_tiles // BUILD, build, (n_near, n_far))
    steps = n_near // UNROLL

    def move(n, n_far):
        order[n_far] = near[n]
        return n_far + 1

    n_far = lax.fori_loop(steps * UNROLL, n_near, move, n_far)
    count[0] = n_far // UNROLL
    pair_sums(near, steps, lists, a, b, p, join, own_tiles, tiles_ext)


def rest_kernel(
    lists, place, order, count, coords, below, above, own_depth, well, radius, hidx, ref, restr, prev, nxt,
    center, b, a_in, p_in, join_in,
    force, sums, a, p, join,
    halo_x, depth_s, radius_s,
):
    images = coords.shape[1]
    own_tiles = own_depth.shape[0]
    tiles_ext = a.shape[0] // images
    halo_tiles = tiles_ext - own_tiles
    side_tiles = halo_tiles // 2
    wells, radii = table(well), table(radius)

    for side, source in enumerate((below, above)):
        low, high = [], []
        for m in range(images):
            idx = jnp.concatenate(
                [hidx[m, side : side + 1, q * TILE : (q + 1) * TILE] for q in range(side_tiles)],
                axis=0,
            )
            low.append(idx & (TILE - 1))
            high.append(idx >> 7)

        def gather_row(r, carry):
            out = []
            for m in range(images):
                hit = high[m] == r
                for c in range(4):
                    wide = jnp.broadcast_to(source[c, m : m + 1, lanes(r)], (8, TILE))
                    out.append(jnp.where(hit, take(wide, low[m]), carry[4 * m + c]))
            return tuple(out)

        zero = jnp.zeros((8, TILE), f32)
        found = lax.fori_loop(0, own_tiles, gather_row, (zero,) * (4 * images), unroll=8)
        inside = place[side].astype(f32)
        spot = slice(side * side_tiles, (side + 1) * side_tiles)
        for m in range(images):
            for c in range(3):
                halo_x[m, c, spot] = found[4 * m + c]
            kind = found[4 * m + 3].astype(jnp.int32)
            depth_s[m, spot] = take(wells, kind) * inside
            radius_s[m, spot] = take(radii, kind)

    for m in range(images):
        middle = center[m, 0:3]

        def build(n, carry):
            made = []
            for h in range(BUILD):
                t = BUILD * n + h
                x3 = jnp.concatenate([halo_x[m, c, pl.ds(t, 1)] for c in range(3)], axis=0)
                made.append(
                    streamed_features(
                        x3 - middle, depth_s[m, pl.ds(t, 1)], radius_s[m, pl.ds(t, 1)]
                    )
                )
            store_tiles(a, p, m * tiles_ext + own_tiles + BUILD * n, made)
            return carry

        lax.fori_loop(0, halo_tiles // BUILD, build, 0)

    pair_sums(order, count[0], lists, a, b, p, join, own_tiles, tiles_ext)

    def finish(n, carry):
        carry = list(carry)
        for h in range(4):
            t = 4 * n + h
            at = lanes(t)
            depth = own_depth[pl.ds(t, 1)]
            stiff = restr[:, at]
            rows = [join[m * own_tiles + t] for m in range(images)]
            weight = jnp.concatenate([r[0:1] for r in rows], axis=0)
            carry[5] += 2.0 * depth * jnp.concatenate([r[4:5] for r in rows], axis=0)
            for c in range(3):
                x = coords[c, :, at]
                middle = jnp.concatenate([center[m, c : c + 1] for m in range(images)], axis=0)
                moved = jnp.concatenate([r[1 + c : 2 + c] for r in rows], axis=0)
                offset = x - ref[c : c + 1, at]
                pull = stiff * offset
                total = 24.0 * depth * ((x - middle) * weight - moved) - pull
                force[c, :, at] = total
                before = jnp.concatenate([prev[c, :, at], x[0:1]], axis=0)
                after = jnp.concatenate([x[1:2], nxt[c, :, at]], axis=0)
                ahead, behind = after - x, x - before
                both_ways, bend = ahead + behind, ahead - behind
                carry[0] += both_ways * both_ways
                carry[1] += both_ways * bend
                carry[2] += bend * bend
                carry[3] += total * both_ways
                carry[4] += total * bend
                carry[5] += 0.5 * pull * offset
        return tuple(carry)

    zero = jnp.zeros((images, TILE), f32)
    line = lax.fori_loop(0, own_tiles // 4, finish, (zero,) * 6)
    line = jnp.concatenate(list(line) + [jnp.zeros((16 - 6 * images, TILE), f32)], axis=0)
    row, lane = rows_of((16, 16)), lax.broadcasted_iota(jnp.int32, (16, 16), 1)
    totals = jnp.sum(line, axis=1, keepdims=True)
    totals = jnp.sum(jnp.where(row == lane, totals, 0.0), axis=0, keepdims=True)
    sums[...] = totals


def band_kernel(place, shares, force, coords, prev, nxt, out, energies):
    total = shares[...]
    images, atoms = coords.shape[1], coords.shape[2]
    parts = []
    for m in range(images):
        s_sq, cross, b_sq, f_s, f_b, energy = [
            total[:, images * n + m : images * n + m + 1] for n in range(6)
        ]
        energies[m] = (energy / (16 * atoms))[0, 0]
        base = 0.25 * (s_sq + b_sq) + small_eps
        ahead_sq, behind_sq = base + 0.5 * cross, base - 0.5 * cross
        ahead_len, behind_len = jnp.sqrt(ahead_sq), jnp.sqrt(behind_sq)
        inverse_sum = 1.0 / ahead_len + 1.0 / behind_len
        alpha = 0.5 * inverse_sum
        beta = -0.5 * cross / (ahead_sq * behind_sq * inverse_sum)
        tan_sq = alpha * alpha * s_sq + 2.0 * alpha * beta * cross + beta * beta * b_sq
        tan_len = jnp.sqrt(jnp.maximum(tan_sq, 0.0) + small_eps)
        along = (alpha * f_s + beta * f_b) / tan_len
        stretch = cross / (ahead_len + behind_len)
        gain = (spring_k * stretch - along) / tan_len
        gain = jnp.where(place[2 + m] == 1, 0.0, gain)
        parts.append((gain * alpha, gain * beta))
    for_s = jnp.concatenate([jnp.broadcast_to(q[0], (1, TILE)) for q in parts], axis=0)
    for_b = jnp.concatenate([jnp.broadcast_to(q[1], (1, TILE)) for q in parts], axis=0)
    for t in range(atoms // TILE):
        at = slice(t * TILE, (t + 1) * TILE)
        for c in range(3):
            x = coords[c, :, at]
            before = jnp.concatenate([prev[c, :, at], x[0:1]], axis=0)
            after = jnp.concatenate([x[1:2], nxt[c, :, at]], axis=0)
            ahead, behind = after - x, x - before
            out[c, :, at] = force[c, :, at] + for_s * (ahead + behind) + for_b * (ahead - behind)


def ring(axis, step):
    n = lax.axis_size(axis)
    return [(i, (i + step) % n) for i in range(n)]


def shape(dims, dtype=f32):
    return jax.ShapeDtypeStruct(dims, dtype)


def params(mib, **more):
    return dict(compiler_params=pltpu.CompilerParams(vmem_limit_bytes=mib << 20), **more)


def body(
    coords, ref_coords, restraint, atom_types, well_table, radius_table, tile_lists, halo_index
):
    images, _, atoms = coords.shape
    tiles = atoms // TILE
    tiles_ext = tiles + 2 * halo_index.shape[2] // TILE
    types = atom_types.reshape(tiles, TILE)
    well, radius = well_table[None], radius_table[None]
    feats, first, last, place = pl.pallas_call(
        prep_kernel,
        out_shape=(
            shape((4, images, atoms)),
            shape((3, 1, atoms)),
            shape((3, 1, atoms)),
            shape((4,), jnp.int32),
        ),
        in_specs=[VMEM] * 2,
        out_specs=(VMEM,) * 3 + (SMEM,),
        cost_estimate=pl.CostEstimate(flops=10**10, bytes_accessed=10**6, transcendentals=0),
        name="prep",
        **params(8),
    )(coords.transpose(1, 0, 2), types)
    below = lax.ppermute(feats, "space", ring("space", 1))
    above = lax.ppermute(feats, "space", ring("space", -1))
    prev = lax.ppermute(last, "image", ring("image", 1))
    nxt = lax.ppermute(first, "image", ring("image", -1))
    own = images * tiles
    a, b, p, join, center, depth, order, count = pl.pallas_call(
        own_kernel,
        out_shape=(
            shape((images * tiles_ext, TILE, TILE), bf16),
            shape((own, TILE, 2 * TILE), bf16),
            shape((images * tiles_ext, 16, TILE), bf16),
            shape((own, 8, TILE)),
            shape((images, 8, TILE)),
            shape((tiles, TILE)),
            shape((own,), jnp.int32),
            shape((1,), jnp.int32),
        ),
        in_specs=[SMEM] * 2 + [VMEM] * 4,
        out_specs=(VMEM,) * 6 + (SMEM,) * 2,
        scratch_shapes=[
            pltpu.SMEM((own,), jnp.int32),
            pltpu.VMEM((tiles, TILE), f32),
        ],
        cost_estimate=pl.CostEstimate(flops=60 * 10**9, bytes_accessed=10**6, transcendentals=0),
        name="own",
        **params(16),
    )(tile_lists, place, feats, types, well, radius)
    force, sums, *_ = pl.pallas_call(
        rest_kernel,
        out_shape=(
            shape((3, images, atoms)),
            shape((1, 16)),
            shape(a.shape, bf16),
            shape(p.shape, bf16),
            shape(join.shape),
        ),
        in_specs=[SMEM] * 4 + [VMEM] * 16,
        out_specs=(VMEM,) * 5,
        input_output_aliases={17: 2, 18: 3, 19: 4},
        scratch_shapes=[
            pltpu.VMEM((images, 3, tiles_ext - tiles, TILE), f32),
            pltpu.VMEM((images, tiles_ext - tiles, TILE), f32),
            pltpu.VMEM((images, tiles_ext - tiles, TILE), f32),
        ],
        name="rest",
        **params(16),
    )(
        tile_lists, place, order, count, feats, below, above, depth, well, radius, halo_index,
        ref_coords, restraint[None], prev, nxt, center, b, a, p, join,
    )
    shares = sums
    for stride in (1, 4):
        parts = [
            lax.ppermute(shares, "space", [(i, i ^ (stride * d)) for i in range(16)])
            for d in (1, 2, 3)
        ]
        shares = shares + (parts[0] + parts[1] + parts[2])
    out, energies = pl.pallas_call(
        band_kernel,
        out_shape=(shape((3, images, atoms)), shape((images,))),
        in_specs=[SMEM] + [VMEM] * 5,
        out_specs=(VMEM, SMEM),
        name="band",
        **params(8),
    )(place, shares, force, feats, prev, nxt)
    return out.transpose(1, 0, 2), energies


def solution(mesh):
    in_specs = (
        P("image", None, "space"),
        P(None, "space"),
        P("space"),
        P("space"),
        P(),
        P(),
        P("image", None, "space"),
        P("image", None, "space"),
    )
    out_specs = (P("image", None, "space"), P("image"))
    return jax.shard_map(body, mesh=mesh, in_specs=in_specs, out_specs=out_specs, check_vma=False)
```

```python
import jax
import jax.numpy as jnp
from jax import lax
from jax.experimental import pallas as pl
from jax.experimental.pallas import tpu as pltpu
from jax.sharding import PartitionSpec as P

TILE = 128
PARTNERS = 4
UNROLL = 32
BUILD = 16
spring_k = 2.0
small_eps = 1e-06
f32, bf16 = jnp.float32, jnp.bfloat16
GROUPS = ((0, 0), (0, 1), (1, 0), (0, 2), (2, 0), (1, 1))
VMEM = pl.BlockSpec(memory_space=pltpu.VMEM)
SMEM = pl.BlockSpec(memory_space=pltpu.SMEM)


def lanes(tile):
    return pl.ds(pl.multiple_of(tile * TILE, TILE), TILE)


def pieces(v):
    first = v.astype(bf16).astype(f32)
    rest = v - first
    second = rest.astype(bf16).astype(f32)
    return first, second, (rest - second).astype(bf16).astype(f32)


def rows_of(shape):
    return lax.broadcasted_iota(jnp.int32, shape, 0)


def streamed_features(x3, depth, radius):
    row = rows_of((8, TILE))
    squares = x3 * x3
    rr = radius * radius
    norm = squares[0:1] + squares[1:2] + squares[2:3] + rr
    cut = pieces(jnp.concatenate([x3, radius, norm, norm, rr, rr], axis=0))
    ones = [jnp.where((row == 5) | (row == 7), 1.0, c) for c in cut]
    streamed = jnp.concatenate([ones[a] for a, _ in GROUPS], axis=0).astype(bf16)
    streamed = jnp.concatenate([streamed, jnp.zeros((16, TILE), bf16)], axis=0)
    moved = jnp.concatenate([depth, depth * x3], axis=0)
    p1, p2, p3 = pieces(jnp.concatenate([moved, moved], axis=0))
    weights = jnp.concatenate(
        [jnp.where(row < 4, p1, p2), jnp.where(row < 4, p3, 0.0)], axis=0
    ).astype(bf16)
    return cut, streamed, weights


def held_features(cut):
    row = rows_of((8, TILE))
    blocks = []
    for a, b in GROUPS:
        own = 1.0 if (a, b) in ((0, 0), (0, 1), (0, 2)) else 0.0
        other = 1.0 if (a, b) in ((0, 0), (1, 0), (2, 0)) else 0.0
        scale_d = jnp.where(row < 3, -2.0, jnp.where(row == 3, 2.0, jnp.where(row == 5, own, 0.0)))
        scale_r = jnp.where(row == 3, 2.0, jnp.where(row == 7, own, 0.0))
        dist = cut[b] * scale_d + jnp.where(row == 4, other, 0.0)
        reach = cut[b] * scale_r + jnp.where(row == 6, other, 0.0)
        blocks.append(jnp.concatenate([dist, reach], axis=1))
    held = jnp.concatenate(blocks, axis=0).astype(bf16)
    rest = jnp.zeros((16, 2 * TILE), bf16)
    return jnp.concatenate([held, rest, held, rest], axis=0)


def store_tiles(a_out, p_out, first, made):
    eye = (rows_of((TILE, TILE)) == lax.broadcasted_iota(jnp.int32, (TILE, TILE), 1)).astype(bf16)
    upper = lax.broadcasted_iota(jnp.int32, (TILE, TILE), 1) >= TILE // 2
    for n in range(0, len(made), 4):
        four = jnp.concatenate([made[n + h][1] for h in range(4)], axis=0)
        turned = lax.dot_general(
            eye, four, (((1,), (1,)), ((), ())), preferred_element_type=f32
        )
        for h in range(4):
            block = turned[:, (h // 2) * TILE : (h // 2 + 1) * TILE]
            block = jnp.where(upper, block, 0.0) if h % 2 else jnp.where(upper, 0.0, block)
            a_out[first + n + h] = block.astype(bf16)
            p_out[first + n + h] = made[n + h][2]


def take(src, idx):
    return jnp.take_along_axis(src, idx, axis=1, mode="promise_in_bounds")


def pair_sums(order, steps, lists, a, b, p, join, own_tiles, tiles_ext):
    def step(n, carry):
        for h in range(UNROLL):
            u = order[n * UNROLL + h]
            m = u // own_tiles
            t = u - m * own_tiles
            held = b[u]
            acc = jnp.zeros((16, 2 * TILE), f32)
            for k in range(PARTNERS):
                q = m * tiles_ext + lists[m, k, t]
                both = jnp.dot(a[q], held, preferred_element_type=f32)
                reach = both[:, TILE:]
                inv = pltpu.reciprocal(both[:, :TILE], approx=True)
                ratio = reach * inv
                cubed = ratio * ratio * ratio
                sixth = cubed * cubed
                energy = sixth - cubed
                coeff = (energy + sixth) * inv
                high = coeff.astype(bf16)
                low = (coeff - high.astype(f32)).astype(bf16)
                left = jnp.concatenate([high, low], axis=0)
                right = jnp.concatenate([energy.astype(bf16), jnp.zeros((TILE, TILE), bf16)], axis=0)
                weights = p[q]
                acc += jnp.dot(
                    jnp.concatenate([weights, weights], axis=1),
                    jnp.concatenate([left, right], axis=1),
                    preferred_element_type=f32,
                )
            joined = acc[0:4] + acc[4:8] + acc[8:12]
            join[u] = jnp.concatenate([joined[:, :TILE], joined[:, TILE:]], axis=0)
        return carry

    lax.fori_loop(0, steps, step, 0)


def table(values):
    wide = jnp.concatenate([values[...], jnp.zeros_like(values[...])], axis=1)
    return jnp.broadcast_to(wide, (8, TILE))


def prep_kernel(coords_in, types, feats, first, last, place):
    images = feats.shape[1]
    slab, image = lax.axis_index("space"), lax.axis_index("image")
    place[0] = (slab > 0).astype(jnp.int32)
    place[1] = (slab < lax.axis_size("space") - 1).astype(jnp.int32)
    place[2] = (image == 0).astype(jnp.int32)
    place[3] = (image == lax.axis_size("image") - 1).astype(jnp.int32)
    for n in range(types.shape[0] // 8):
        kind = types[8 * n : 8 * n + 8].astype(f32)
        for h in range(8):
            t = 8 * n + h
            feats[3, :, t * TILE : (t + 1) * TILE] = jnp.broadcast_to(
                kind[h : h + 1], (images, TILE)
            )
    for c in range(3):
        rows = coords_in[c]
        feats[c] = rows
        first[c] = rows[0:1]
        last[c] = rows[images - 1 : images]


def own_kernel(
    lists, place, coords, types, well, radius,
    a, b, p, join, center, depth_s, order, count,
    near, radius_s,
):
    images = coords.shape[1]
    own_tiles = types.shape[0]
    tiles_ext = a.shape[0] // images
    wells, radii = table(well), table(radius)
    for n in range(own_tiles // 8):
        kind = types[8 * n : 8 * n + 8]
        depth_s[8 * n : 8 * n + 8] = take(wells, kind)
        radius_s[8 * n : 8 * n + 8] = take(radii, kind)
    for c in range(3):
        total = coords[c, :, 0:TILE]
        for t in range(1, own_tiles):
            total = total + coords[c, :, t * TILE : (t + 1) * TILE]
        middle = jnp.sum(total, axis=1, keepdims=True) * (1.0 / (own_tiles * TILE))
        for m in range(images):
            center[m, c : c + 1] = jnp.broadcast_to(middle[m : m + 1], (1, TILE))

    n_near, n_far = jnp.int32(0), jnp.int32(0)
    for m in range(images):
        middle = center[m, 0:3]

        def build(n, carry):
            n_near, n_far = carry
            made = []
            for h in range(BUILD):
                t = BUILD * n + h
                u = m * own_tiles + t
                x3 = jnp.concatenate([coords[c, m : m + 1, lanes(t)] for c in range(3)], axis=0)
                made.append(
                    streamed_features(x3 - middle, depth_s[pl.ds(t, 1)], radius_s[pl.ds(t, 1)])
                )
                b[u] = held_features(made[-1][0])
                last = lists[m, 0, t]
                for k in range(1, PARTNERS):
                    last = jnp.maximum(last, lists[m, k, t])
                inside = (last < own_tiles).astype(jnp.int32)
                near[n_near] = u
                order[n_far] = u
                n_near = n_near + inside
                n_far = n_far + (1 - inside)
            store_tiles(a, p, m * tiles_ext + BUILD * n, made)
            return n_near, n_far

        n_near, n_far = lax.fori_loop(0, own_tiles // BUILD, build, (n_near, n_far))
    steps = n_near // UNROLL

    def move(n, n_far):
        order[n_far] = near[n]
        return n_far + 1

    n_far = lax.fori_loop(steps * UNROLL, n_near, move, n_far)
    count[0] = n_far // UNROLL
    pair_sums(near, steps, lists, a, b, p, join, own_tiles, tiles_ext)


def rest_kernel(
    lists, place, order, count, coords, below, above, own_depth, well, radius, hidx, ref, restr, prev, nxt,
    center, b, a_in, p_in, join_in,
    force, slope, bending, sums, a, p, join,
    halo_x, depth_s, radius_s,
):
    images = coords.shape[1]
    own_tiles = own_depth.shape[0]
    tiles_ext = a.shape[0] // images
    halo_tiles = tiles_ext - own_tiles
    side_tiles = halo_tiles // 2
    wells, radii = table(well), table(radius)

    for side, source in enumerate((below, above)):
        low, high = [], []
        for m in range(images):
            idx = jnp.concatenate(
                [hidx[m, side : side + 1, q * TILE : (q + 1) * TILE] for q in range(side_tiles)],
                axis=0,
            )
            low.append(idx & (TILE - 1))
            high.append(idx >> 7)

        def gather_row(r, carry):
            out = []
            for m in range(images):
                hit = high[m] == r
                for c in range(4):
                    wide = jnp.broadcast_to(source[c, m : m + 1, lanes(r)], (8, TILE))
                    out.append(jnp.where(hit, take(wide, low[m]), carry[4 * m + c]))
            return tuple(out)

        zero = jnp.zeros((8, TILE), f32)
        found = lax.fori_loop(0, own_tiles, gather_row, (zero,) * (4 * images), unroll=8)
        inside = place[side].astype(f32)
        spot = slice(side * side_tiles, (side + 1) * side_tiles)
        for m in range(images):
            for c in range(3):
                halo_x[m, c, spot] = found[4 * m + c]
            kind = found[4 * m + 3].astype(jnp.int32)
            depth_s[m, spot] = take(wells, kind) * inside
            radius_s[m, spot] = take(radii, kind)

    for m in range(images):
        middle = center[m, 0:3]

        def build(n, carry):
            made = []
            for h in range(BUILD):
                t = BUILD * n + h
                x3 = jnp.concatenate([halo_x[m, c, pl.ds(t, 1)] for c in range(3)], axis=0)
                made.append(
                    streamed_features(
                        x3 - middle, depth_s[m, pl.ds(t, 1)], radius_s[m, pl.ds(t, 1)]
                    )
                )
            store_tiles(a, p, m * tiles_ext + own_tiles + BUILD * n, made)
            return carry

        lax.fori_loop(0, halo_tiles // BUILD, build, 0)

    pair_sums(order, count[0], lists, a, b, p, join, own_tiles, tiles_ext)

    def finish(n, carry):
        carry = list(carry)
        for h in range(8):
            t = 8 * n + h
            at = lanes(t)
            depth = own_depth[pl.ds(t, 1)]
            stiff = restr[:, at]
            rows = [join[m * own_tiles + t] for m in range(images)]
            weight = jnp.concatenate([r[0:1] for r in rows], axis=0)
            carry[5] += 2.0 * depth * jnp.concatenate([r[4:5] for r in rows], axis=0)
            for c in range(3):
                x = coords[c, :, at]
                middle = jnp.concatenate([center[m, c : c + 1] for m in range(images)], axis=0)
                moved = jnp.concatenate([r[1 + c : 2 + c] for r in rows], axis=0)
                offset = x - ref[c : c + 1, at]
                pull = stiff * offset
                total = 24.0 * depth * ((x - middle) * weight - moved) - pull
                force[c, :, at] = total
                before = jnp.concatenate([prev[c, :, at], x[0:1]], axis=0)
                after = jnp.concatenate([x[1:2], nxt[c, :, at]], axis=0)
                ahead, behind = after - x, x - before
                both_ways, bend = ahead + behind, ahead - behind
                slope[c, :, at] = both_ways
                bending[c, :, at] = bend
                carry[0] += both_ways * both_ways
                carry[1] += both_ways * bend
                carry[2] += bend * bend
                carry[3] += total * both_ways
                carry[4] += total * bend
                carry[5] += 0.5 * pull * offset
        return tuple(carry)

    zero = jnp.zeros((images, TILE), f32)
    line = lax.fori_loop(0, own_tiles // 8, finish, (zero,) * 6)
    line = jnp.concatenate(list(line) + [jnp.zeros((16 - 6 * images, TILE), f32)], axis=0)
    row, lane = rows_of((16, 16)), lax.broadcasted_iota(jnp.int32, (16, 16), 1)
    totals = jnp.sum(line, axis=1, keepdims=True)
    totals = jnp.sum(jnp.where(row == lane, totals, 0.0), axis=0, keepdims=True)
    sums[...] = jnp.broadcast_to(totals, (16, 16))


def band_kernel(place, shares, force, slope, bending, out, energies):
    total = jnp.sum(shares[...], axis=0, keepdims=True)
    images, atoms = force.shape[1], force.shape[2]
    parts = []
    for m in range(images):
        s_sq, cross, b_sq, f_s, f_b, energy = [
            total[:, images * n + m : images * n + m + 1] for n in range(6)
        ]
        energies[m] = (energy / (16 * atoms))[0, 0]
        base = 0.25 * (s_sq + b_sq) + small_eps
        ahead_sq, behind_sq = base + 0.5 * cross, base - 0.5 * cross
        ahead_len, behind_len = jnp.sqrt(ahead_sq), jnp.sqrt(behind_sq)
        inverse_sum = 1.0 / ahead_len + 1.0 / behind_len
        alpha = 0.5 * inverse_sum
        beta = -0.5 * cross / (ahead_sq * behind_sq * inverse_sum)
        tan_sq = alpha * alpha * s_sq + 2.0 * alpha * beta * cross + beta * beta * b_sq
        tan_len = jnp.sqrt(jnp.maximum(tan_sq, 0.0) + small_eps)
        along = (alpha * f_s + beta * f_b) / tan_len
        stretch = cross / (ahead_len + behind_len)
        gain = (spring_k * stretch - along) / tan_len
        gain = jnp.where(place[2 + m] == 1, 0.0, gain)
        parts.append((gain * alpha, gain * beta))
    for_s = jnp.concatenate([jnp.broadcast_to(q[0], (1, TILE)) for q in parts], axis=0)
    for_b = jnp.concatenate([jnp.broadcast_to(q[1], (1, TILE)) for q in parts], axis=0)
    for t in range(atoms // TILE):
        at = slice(t * TILE, (t + 1) * TILE)
        for c in range(3):
            out[c, :, at] = force[c, :, at] + for_s * slope[c, :, at] + for_b * bending[c, :, at]


def ring(axis, step):
    n = lax.axis_size(axis)
    return [(i, (i + step) % n) for i in range(n)]


def shape(dims, dtype=f32):
    return jax.ShapeDtypeStruct(dims, dtype)


def params(mib, **more):
    return dict(compiler_params=pltpu.CompilerParams(vmem_limit_bytes=mib << 20), **more)


def body(
    coords, ref_coords, restraint, atom_types, well_table, radius_table, tile_lists, halo_index
):
    images, _, atoms = coords.shape
    tiles = atoms // TILE
    tiles_ext = tiles + 2 * halo_index.shape[2] // TILE
    types = atom_types.reshape(tiles, TILE)
    well, radius = well_table[None], radius_table[None]
    feats, first, last, place = pl.pallas_call(
        prep_kernel,
        out_shape=(
            shape((4, images, atoms)),
            shape((3, 1, atoms)),
            shape((3, 1, atoms)),
            shape((4,), jnp.int32),
        ),
        in_specs=[VMEM] * 2,
        out_specs=(VMEM,) * 3 + (SMEM,),
        cost_estimate=pl.CostEstimate(flops=10**10, bytes_accessed=10**6, transcendentals=0),
        name="prep",
        **params(8),
    )(coords.transpose(1, 0, 2), types)
    below = lax.ppermute(feats, "space", ring("space", 1))
    above = lax.ppermute(feats, "space", ring("space", -1))
    prev = lax.ppermute(last, "image", ring("image", 1))
    nxt = lax.ppermute(first, "image", ring("image", -1))
    own = images * tiles
    a, b, p, join, center, depth, order, count = pl.pallas_call(
        own_kernel,
        out_shape=(
            shape((images * tiles_ext, TILE, TILE), bf16),
            shape((own, TILE, 2 * TILE), bf16),
            shape((images * tiles_ext, 16, TILE), bf16),
            shape((own, 8, TILE)),
            shape((images, 8, TILE)),
            shape((tiles, TILE)),
            shape((own,), jnp.int32),
            shape((1,), jnp.int32),
        ),
        in_specs=[SMEM] * 2 + [VMEM] * 4,
        out_specs=(VMEM,) * 6 + (SMEM,) * 2,
        scratch_shapes=[
            pltpu.SMEM((own,), jnp.int32),
            pltpu.VMEM((tiles, TILE), f32),
        ],
        cost_estimate=pl.CostEstimate(flops=60 * 10**9, bytes_accessed=10**6, transcendentals=0),
        name="own",
        **params(16),
    )(tile_lists, place, feats, types, well, radius)
    force, slope, bending, sums, *_ = pl.pallas_call(
        rest_kernel,
        out_shape=(
            shape((3, images, atoms)),
            shape((3, images, atoms)),
            shape((3, images, atoms)),
            shape((16, 16)),
            shape(a.shape, bf16),
            shape(p.shape, bf16),
            shape(join.shape),
        ),
        in_specs=[SMEM] * 4 + [VMEM] * 16,
        out_specs=(VMEM,) * 7,
        input_output_aliases={17: 4, 18: 5, 19: 6},
        scratch_shapes=[
            pltpu.VMEM((images, 3, tiles_ext - tiles, TILE), f32),
            pltpu.VMEM((images, tiles_ext - tiles, TILE), f32),
            pltpu.VMEM((images, tiles_ext - tiles, TILE), f32),
        ],
        name="rest",
        **params(16),
    )(
        tile_lists, place, order, count, feats, below, above, depth, well, radius, halo_index,
        ref_coords, restraint[None], prev, nxt, center, b, a, p, join,
    )
    shares = lax.all_to_all(sums, "space", 0, 0, tiled=True)
    out, energies = pl.pallas_call(
        band_kernel,
        out_shape=(shape((3, images, atoms)), shape((images,))),
        in_specs=[SMEM] + [VMEM] * 4,
        out_specs=(VMEM, SMEM),
        name="band",
        **params(8),
    )(place, shares, force, slope, bending)
    return out.transpose(1, 0, 2), energies


def solution(mesh):
    in_specs = (
        P("image", None, "space"),
        P(None, "space"),
        P("space"),
        P("space"),
        P(),
        P(),
        P("image", None, "space"),
        P("image", None, "space"),
    )
    out_specs = (P("image", None, "space"), P("image"))
    return jax.shard_map(body, mesh=mesh, in_specs=in_specs, out_specs=out_specs, check_vma=False)
```

```python
import jax
import jax.numpy as jnp
from jax import lax
from jax.experimental import pallas as pl
from jax.experimental.pallas import tpu as pltpu
from jax.sharding import PartitionSpec as P

TILE = 128
PARTNERS = 4
BLOCK = 16
BUILD = 16
spring_k = 2.0
small_eps = 1e-06
f32, bf16 = jnp.float32, jnp.bfloat16
GROUPS = ((0, 0), (0, 1), (1, 0), (0, 2), (2, 0), (1, 1))
VMEM = pl.BlockSpec(memory_space=pltpu.VMEM)
SMEM = pl.BlockSpec(memory_space=pltpu.SMEM)


def lanes(tile):
    return pl.ds(pl.multiple_of(tile * TILE, TILE), TILE)


def pieces(v):
    first = v.astype(bf16).astype(f32)
    rest = v - first
    second = rest.astype(bf16).astype(f32)
    return first, second, (rest - second).astype(bf16).astype(f32)


def rows_of(shape):
    return lax.broadcasted_iota(jnp.int32, shape, 0)


def streamed_features(x, y, z, depth, radius):
    row = rows_of((8, TILE))
    rr = radius * radius
    norm = x * x + y * y + z * z + rr
    base = jnp.where(row == 3, radius, jnp.where(row < 6, norm, rr))
    cut = pieces(jnp.where(row == 0, x, jnp.where(row == 1, y, jnp.where(row == 2, z, base))))
    ones = [jnp.where((row == 5) | (row == 7), 1.0, c) for c in cut]
    streamed = jnp.concatenate([ones[a] for a, _ in GROUPS], axis=0).astype(bf16)
    streamed = jnp.concatenate([streamed, jnp.zeros((16, TILE), bf16)], axis=0)
    quarter = row & 3
    moved = jnp.where(quarter == 0, 1.0, jnp.where(quarter == 1, x, jnp.where(quarter == 2, y, z)))
    p1, p2, p3 = pieces(depth * moved)
    weights = jnp.concatenate(
        [jnp.where(row < 4, p1, p2), jnp.where(row < 4, p3, 0.0)], axis=0
    ).astype(bf16)
    return cut, streamed, weights


def repeated(row):
    return jnp.broadcast_to(row, (8, TILE))


def held_features(cut):
    row = rows_of((8, TILE))
    blocks = []
    for a, b in GROUPS:
        own = 1.0 if (a, b) in ((0, 0), (0, 1), (0, 2)) else 0.0
        other = 1.0 if (a, b) in ((0, 0), (1, 0), (2, 0)) else 0.0
        scale_d = jnp.where(row < 3, -2.0, jnp.where(row == 3, 2.0, jnp.where(row == 5, own, 0.0)))
        scale_r = jnp.where(row == 3, 2.0, jnp.where(row == 7, own, 0.0))
        dist = cut[b] * scale_d + jnp.where(row == 4, other, 0.0)
        reach = cut[b] * scale_r + jnp.where(row == 6, other, 0.0)
        blocks.append(jnp.concatenate([dist, reach], axis=1))
    held = jnp.concatenate(blocks, axis=0).astype(bf16)
    rest = jnp.zeros((16, 2 * TILE), bf16)
    return jnp.concatenate([held, rest, held, rest], axis=0)


def store_tiles(a_out, p_out, first, made):
    eye = (rows_of((TILE, TILE)) == lax.broadcasted_iota(jnp.int32, (TILE, TILE), 1)).astype(bf16)
    upper = lax.broadcasted_iota(jnp.int32, (TILE, TILE), 1) >= TILE // 2
    for n in range(0, len(made), 4):
        four = jnp.concatenate([made[n + h][1] for h in range(4)], axis=0)
        turned = lax.dot_general(
            eye, four, (((1,), (1,)), ((), ())), preferred_element_type=f32
        )
        for h in range(4):
            block = turned[:, (h // 2) * TILE : (h // 2 + 1) * TILE]
            block = jnp.where(upper, block, 0.0) if h % 2 else jnp.where(upper, 0.0, block)
            a_out[first + n + h] = block.astype(bf16)
            p_out[first + n + h] = made[n + h][2]


def take(src, idx):
    return jnp.take_along_axis(src, idx, axis=1, mode="promise_in_bounds")


def pair_sums(order, blocks, lists, a, b, p, join, own_tiles, tiles_ext):
    def step(first, tiles, carry):
        for h in range(tiles):
            u = order[first + h]
            m = u // own_tiles
            t = u - m * own_tiles
            held = b[u]
            acc = jnp.zeros((16, 2 * TILE), f32)
            for k in range(PARTNERS):
                q = m * tiles_ext + lists[m, k, t]
                both = jnp.dot(a[q], held, preferred_element_type=f32)
                reach = both[:, TILE:]
                inv = pltpu.reciprocal(both[:, :TILE], approx=True)
                ratio = reach * inv
                cubed = ratio * ratio * ratio
                sixth = cubed * cubed
                energy = sixth - cubed
                coeff = (energy + sixth) * inv
                high = coeff.astype(bf16)
                low = (coeff - high.astype(f32)).astype(bf16)
                left = jnp.concatenate([high, low], axis=0)
                right = jnp.concatenate([energy.astype(bf16), jnp.zeros((TILE, TILE), bf16)], axis=0)
                weights = p[q]
                acc += jnp.dot(
                    jnp.concatenate([weights, weights], axis=1),
                    jnp.concatenate([left, right], axis=1),
                    preferred_element_type=f32,
                )
            joined = acc[0:4] + acc[4:8] + acc[8:12]
            join[u] = jnp.concatenate([joined[:, :TILE], joined[:, TILE:]], axis=0)
        return carry

    pairs = blocks // 2
    lax.fori_loop(0, pairs, lambda n, c: step(n * (2 * BLOCK), 2 * BLOCK, c), 0)
    lax.fori_loop(2 * pairs, blocks, lambda n, c: step(n * BLOCK, BLOCK, c), 0)


def table(values):
    wide = jnp.concatenate([values[...], jnp.zeros_like(values[...])], axis=1)
    return jnp.broadcast_to(wide, (8, TILE))


def prep_kernel(coords_in, types, feats, first, last, place):
    images = feats.shape[1]
    slab, image = lax.axis_index("space"), lax.axis_index("image")
    place[0] = (slab > 0).astype(jnp.int32)
    place[1] = (slab < lax.axis_size("space") - 1).astype(jnp.int32)
    place[2] = (image == 0).astype(jnp.int32)
    place[3] = (image == lax.axis_size("image") - 1).astype(jnp.int32)
    for n in range(types.shape[0] // 8):
        kind = types[8 * n : 8 * n + 8].astype(f32)
        for h in range(8):
            t = 8 * n + h
            feats[3, :, t * TILE : (t + 1) * TILE] = jnp.broadcast_to(
                kind[h : h + 1], (images, TILE)
            )
    for c in range(3):
        rows = coords_in[c]
        feats[c] = rows
        first[c] = rows[0:1]
        last[c] = rows[images - 1 : images]


def own_kernel(
    lists, place, coords, types, well, radius,
    a, b, p, join, center, depth_s, order, count,
    near, radius_s,
):
    images = coords.shape[1]
    own_tiles = types.shape[0]
    tiles_ext = a.shape[0] // images
    wells, radii = table(well), table(radius)
    for n in range(own_tiles // 8):
        kind = types[8 * n : 8 * n + 8]
        depth_s[8 * n : 8 * n + 8] = take(wells, kind)
        radius_s[8 * n : 8 * n + 8] = take(radii, kind)
    for c in range(3):
        total = coords[c, :, 0:TILE]
        for t in range(1, own_tiles):
            total = total + coords[c, :, t * TILE : (t + 1) * TILE]
        middle = jnp.sum(total, axis=1, keepdims=True) * (1.0 / (own_tiles * TILE))
        for m in range(images):
            center[m, c : c + 1] = jnp.broadcast_to(middle[m : m + 1], (1, TILE))

    n_near, n_far = jnp.int32(0), jnp.int32(0)
    for m in range(images):
        middle = [repeated(center[m, c : c + 1]) for c in range(3)]

        def build(n, carry):
            n_near, n_far = carry
            made = []
            for h in range(BUILD):
                t = BUILD * n + h
                u = m * own_tiles + t
                xyz = [repeated(coords[c, m : m + 1, lanes(t)]) - middle[c] for c in range(3)]
                made.append(
                    streamed_features(
                        *xyz, repeated(depth_s[pl.ds(t, 1)]), repeated(radius_s[pl.ds(t, 1)])
                    )
                )
                b[u] = held_features(made[-1][0])
                last = lists[m, 0, t]
                for k in range(1, PARTNERS):
                    last = jnp.maximum(last, lists[m, k, t])
                inside = (last < own_tiles).astype(jnp.int32)
                near[n_near] = u
                order[n_far] = u
                n_near = n_near + inside
                n_far = n_far + (1 - inside)
            store_tiles(a, p, m * tiles_ext + BUILD * n, made)
            return n_near, n_far

        n_near, n_far = lax.fori_loop(0, own_tiles // BUILD, build, (n_near, n_far))
    blocks = n_near // BLOCK

    def move(n, n_far):
        order[n_far] = near[n]
        return n_far + 1

    n_far = lax.fori_loop(blocks * BLOCK, n_near, move, n_far)
    count[0] = n_far // BLOCK
    pair_sums(near, blocks, lists, a, b, p, join, own_tiles, tiles_ext)


def rest_kernel(
    lists, place, order, count, coords, below, above, own_depth, well, radius, hidx, ref, restr, prev, nxt,
    center, b, a_in, p_in, join_in,
    force, slope, bending, sums, a, p, join,
    halo_x, depth_s, radius_s,
):
    images = coords.shape[1]
    own_tiles = own_depth.shape[0]
    tiles_ext = a.shape[0] // images
    halo_tiles = tiles_ext - own_tiles
    side_tiles = halo_tiles // 2
    wells, radii = table(well), table(radius)

    for side, source in enumerate((below, above)):
        low, high = [], []
        for m in range(images):
            idx = jnp.concatenate(
                [hidx[m, side : side + 1, q * TILE : (q + 1) * TILE] for q in range(side_tiles)],
                axis=0,
            )
            low.append(idx & (TILE - 1))
            high.append(idx >> 7)

        def gather_row(r, carry):
            out = []
            for m in range(images):
                hit = high[m] == r
                for c in range(4):
                    wide = jnp.broadcast_to(source[c, m : m + 1, lanes(r)], (8, TILE))
                    out.append(jnp.where(hit, take(wide, low[m]), carry[4 * m + c]))
            return tuple(out)

        zero = jnp.zeros((8, TILE), f32)
        found = lax.fori_loop(0, own_tiles, gather_row, (zero,) * (4 * images), unroll=8)
        inside = place[side].astype(f32)
        spot = slice(side * side_tiles, (side + 1) * side_tiles)
        for m in range(images):
            for c in range(3):
                halo_x[m, c, spot] = found[4 * m + c]
            kind = found[4 * m + 3].astype(jnp.int32)
            depth_s[m, spot] = take(wells, kind) * inside
            radius_s[m, spot] = take(radii, kind)

    for m in range(images):
        middle = [repeated(center[m, c : c + 1]) for c in range(3)]

        def build(n, carry):
            made = []
            for h in range(BUILD):
                t = BUILD * n + h
                xyz = [repeated(halo_x[m, c, pl.ds(t, 1)]) - middle[c] for c in range(3)]
                made.append(
                    streamed_features(
                        *xyz, repeated(depth_s[m, pl.ds(t, 1)]), repeated(radius_s[m, pl.ds(t, 1)])
                    )
                )
            store_tiles(a, p, m * tiles_ext + own_tiles + BUILD * n, made)
            return carry

        lax.fori_loop(0, halo_tiles // BUILD, build, 0)

    pair_sums(order, count[0], lists, a, b, p, join, own_tiles, tiles_ext)

    def finish(n, carry):
        carry = list(carry)
        for h in range(8):
            t = 8 * n + h
            at = lanes(t)
            depth = own_depth[pl.ds(t, 1)]
            stiff = restr[:, at]
            rows = [join[m * own_tiles + t] for m in range(images)]
            weight = jnp.concatenate([r[0:1] for r in rows], axis=0)
            carry[5] += 2.0 * depth * jnp.concatenate([r[4:5] for r in rows], axis=0)
            for c in range(3):
                x = coords[c, :, at]
                middle = jnp.concatenate([center[m, c : c + 1] for m in range(images)], axis=0)
                moved = jnp.concatenate([r[1 + c : 2 + c] for r in rows], axis=0)
                offset = x - ref[c : c + 1, at]
                pull = stiff * offset
                total = 24.0 * depth * ((x - middle) * weight - moved) - pull
                force[c, :, at] = total
                before = jnp.concatenate([prev[c, :, at], x[0:1]], axis=0)
                after = jnp.concatenate([x[1:2], nxt[c, :, at]], axis=0)
                ahead, behind = after - x, x - before
                both_ways, bend = ahead + behind, ahead - behind
                slope[c, :, at] = both_ways
                bending[c, :, at] = bend
                carry[0] += both_ways * both_ways
                carry[1] += both_ways * bend
                carry[2] += bend * bend
                carry[3] += total * both_ways
                carry[4] += total * bend
                carry[5] += 0.5 * pull * offset
        return tuple(carry)

    zero = jnp.zeros((images, TILE), f32)
    line = lax.fori_loop(0, own_tiles // 8, finish, (zero,) * 6)
    line = jnp.concatenate(list(line) + [jnp.zeros((16 - 6 * images, TILE), f32)], axis=0)
    row, lane = rows_of((16, 16)), lax.broadcasted_iota(jnp.int32, (16, 16), 1)
    totals = jnp.sum(line, axis=1, keepdims=True)
    totals = jnp.sum(jnp.where(row == lane, totals, 0.0), axis=0, keepdims=True)
    sums[...] = jnp.broadcast_to(totals, (16, 16))


def band_kernel(place, shares, force, slope, bending, out, energies):
    total = jnp.sum(shares[...], axis=0, keepdims=True)
    images, atoms = force.shape[1], force.shape[2]
    parts = []
    for m in range(images):
        s_sq, cross, b_sq, f_s, f_b, energy = [
            total[:, images * n + m : images * n + m + 1] for n in range(6)
        ]
        energies[m] = (energy / (16 * atoms))[0, 0]
        base = 0.25 * (s_sq + b_sq) + small_eps
        ahead_sq, behind_sq = base + 0.5 * cross, base - 0.5 * cross
        ahead_len, behind_len = jnp.sqrt(ahead_sq), jnp.sqrt(behind_sq)
        inverse_sum = 1.0 / ahead_len + 1.0 / behind_len
        alpha = 0.5 * inverse_sum
        beta = -0.5 * cross / (ahead_sq * behind_sq * inverse_sum)
        tan_sq = alpha * alpha * s_sq + 2.0 * alpha * beta * cross + beta * beta * b_sq
        tan_len = jnp.sqrt(jnp.maximum(tan_sq, 0.0) + small_eps)
        along = (alpha * f_s + beta * f_b) / tan_len
        stretch = cross / (ahead_len + behind_len)
        gain = (spring_k * stretch - along) / tan_len
        gain = jnp.where(place[2 + m] == 1, 0.0, gain)
        parts.append((gain * alpha, gain * beta))
    for_s = jnp.concatenate([jnp.broadcast_to(q[0], (1, TILE)) for q in parts], axis=0)
    for_b = jnp.concatenate([jnp.broadcast_to(q[1], (1, TILE)) for q in parts], axis=0)
    for t in range(atoms // TILE):
        at = slice(t * TILE, (t + 1) * TILE)
        for c in range(3):
            out[c, :, at] = force[c, :, at] + for_s * slope[c, :, at] + for_b * bending[c, :, at]


def ring(axis, step):
    n = lax.axis_size(axis)
    return [(i, (i + step) % n) for i in range(n)]


def shape(dims, dtype=f32):
    return jax.ShapeDtypeStruct(dims, dtype)


def params(mib, **more):
    return dict(compiler_params=pltpu.CompilerParams(vmem_limit_bytes=mib << 20), **more)


def body(
    coords, ref_coords, restraint, atom_types, well_table, radius_table, tile_lists, halo_index
):
    images, _, atoms = coords.shape
    tiles = atoms // TILE
    tiles_ext = tiles + 2 * halo_index.shape[2] // TILE
    types = atom_types.reshape(tiles, TILE)
    well, radius = well_table[None], radius_table[None]
    feats, first, last, place = pl.pallas_call(
        prep_kernel,
        out_shape=(
            shape((4, images, atoms)),
            shape((3, 1, atoms)),
            shape((3, 1, atoms)),
            shape((4,), jnp.int32),
        ),
        in_specs=[VMEM] * 2,
        out_specs=(VMEM,) * 3 + (SMEM,),
        cost_estimate=pl.CostEstimate(flops=10**10, bytes_accessed=10**6, transcendentals=0),
        name="prep",
        **params(8),
    )(coords.transpose(1, 0, 2), types)
    below = lax.ppermute(feats, "space", ring("space", 1))
    above = lax.ppermute(feats, "space", ring("space", -1))
    prev = lax.ppermute(last, "image", ring("image", 1))
    nxt = lax.ppermute(first, "image", ring("image", -1))
    own = images * tiles
    a, b, p, join, center, depth, order, count = pl.pallas_call(
        own_kernel,
        out_shape=(
            shape((images * tiles_ext, TILE, TILE), bf16),
            shape((own, TILE, 2 * TILE), bf16),
            shape((images * tiles_ext, 16, TILE), bf16),
            shape((own, 8, TILE)),
            shape((images, 8, TILE)),
            shape((tiles, TILE)),
            shape((own,), jnp.int32),
            shape((1,), jnp.int32),
        ),
        in_specs=[SMEM] * 2 + [VMEM] * 4,
        out_specs=(VMEM,) * 6 + (SMEM,) * 2,
        scratch_shapes=[
            pltpu.SMEM((own,), jnp.int32),
            pltpu.VMEM((tiles, TILE), f32),
        ],
        cost_estimate=pl.CostEstimate(flops=60 * 10**9, bytes_accessed=10**6, transcendentals=0),
        name="own",
        **params(16),
    )(tile_lists, place, feats, types, well, radius)
    force, slope, bending, sums, *_ = pl.pallas_call(
        rest_kernel,
        out_shape=(
            shape((3, images, atoms)),
            shape((3, images, atoms)),
            shape((3, images, atoms)),
            shape((16, 16)),
            shape(a.shape, bf16),
            shape(p.shape, bf16),
            shape(join.shape),
        ),
        in_specs=[SMEM] * 4 + [VMEM] * 16,
        out_specs=(VMEM,) * 7,
        input_output_aliases={17: 4, 18: 5, 19: 6},
        scratch_shapes=[
            pltpu.VMEM((images, 3, tiles_ext - tiles, TILE), f32),
            pltpu.VMEM((images, tiles_ext - tiles, TILE), f32),
            pltpu.VMEM((images, tiles_ext - tiles, TILE), f32),
        ],
        name="rest",
        **params(16),
    )(
        tile_lists, place, order, count, feats, below, above, depth, well, radius, halo_index,
        ref_coords, restraint[None], prev, nxt, center, b, a, p, join,
    )
    shares = lax.all_to_all(sums, "space", 0, 0, tiled=True)
    out, energies = pl.pallas_call(
        band_kernel,
        out_shape=(shape((3, images, atoms)), shape((images,))),
        in_specs=[SMEM] + [VMEM] * 4,
        out_specs=(VMEM, SMEM),
        name="band",
        **params(8),
    )(place, shares, force, slope, bending)
    return out.transpose(1, 0, 2), energies


def solution(mesh):
    in_specs = (
        P("image", None, "space"),
        P(None, "space"),
        P("space"),
        P("space"),
        P(),
        P(),
        P("image", None, "space"),
        P("image", None, "space"),
    )
    out_specs = (P("image", None, "space"), P("image"))
    return jax.shard_map(body, mesh=mesh, in_specs=in_specs, out_specs=out_specs, check_vma=False)
```

```python
import jax
import jax.numpy as jnp
from jax import lax
from jax.experimental import pallas as pl
from jax.experimental.pallas import tpu as pltpu
from jax.sharding import PartitionSpec as P

TILE = 128
PARTNERS = 4
BLOCK = 16
BUILD = 16
OWN_BUILD = 32
spring_k = 2.0
small_eps = 1e-06
f32, bf16 = jnp.float32, jnp.bfloat16
GROUPS = ((0, 0), (0, 1), (1, 0), (0, 2), (2, 0), (1, 1))
VMEM = pl.BlockSpec(memory_space=pltpu.VMEM)
SMEM = pl.BlockSpec(memory_space=pltpu.SMEM)


def lanes(tile):
    return pl.ds(pl.multiple_of(tile * TILE, TILE), TILE)


def pieces(v):
    first = v.astype(bf16).astype(f32)
    rest = v - first
    second = rest.astype(bf16).astype(f32)
    return first, second, (rest - second).astype(bf16).astype(f32)


def rows_of(shape):
    return lax.broadcasted_iota(jnp.int32, shape, 0)


def streamed_features(x, y, z, depth, radius):
    row = rows_of((8, TILE))
    rr = radius * radius
    norm = x * x + y * y + z * z + rr
    base = jnp.where(row == 3, radius, jnp.where(row < 6, norm, rr))
    cut = pieces(jnp.where(row == 0, x, jnp.where(row == 1, y, jnp.where(row == 2, z, base))))
    ones = [jnp.where((row == 5) | (row == 7), 1.0, c) for c in cut]
    streamed = jnp.concatenate([ones[a] for a, _ in GROUPS], axis=0).astype(bf16)
    streamed = jnp.concatenate([streamed, jnp.zeros((16, TILE), bf16)], axis=0)
    quarter = row & 3
    moved = jnp.where(quarter == 0, 1.0, jnp.where(quarter == 1, x, jnp.where(quarter == 2, y, z)))
    p1, p2, p3 = pieces(depth * moved)
    weights = jnp.concatenate(
        [jnp.where(row < 4, p1, p2), jnp.where(row < 4, p3, 0.0)], axis=0
    ).astype(bf16)
    return cut, streamed, weights


def repeated(row):
    return jnp.broadcast_to(row, (8, TILE))


def held_features(cut):
    row = rows_of((8, TILE))
    blocks = []
    for a, b in GROUPS:
        own = 1.0 if (a, b) in ((0, 0), (0, 1), (0, 2)) else 0.0
        other = 1.0 if (a, b) in ((0, 0), (1, 0), (2, 0)) else 0.0
        scale_d = jnp.where(row < 3, -2.0, jnp.where(row == 3, 2.0, jnp.where(row == 5, own, 0.0)))
        scale_r = jnp.where(row == 3, 2.0, jnp.where(row == 7, own, 0.0))
        dist = cut[b] * scale_d + jnp.where(row == 4, other, 0.0)
        reach = cut[b] * scale_r + jnp.where(row == 6, other, 0.0)
        blocks.append(jnp.concatenate([dist, reach], axis=1))
    held = jnp.concatenate(blocks, axis=0).astype(bf16)
    rest = jnp.zeros((16, 2 * TILE), bf16)
    return jnp.concatenate([held, rest, held, rest], axis=0)


def store_tiles(a_out, p_out, first, made):
    eye = (rows_of((TILE, TILE)) == lax.broadcasted_iota(jnp.int32, (TILE, TILE), 1)).astype(bf16)
    upper = lax.broadcasted_iota(jnp.int32, (TILE, TILE), 1) >= TILE // 2
    for n in range(0, len(made), 4):
        four = jnp.concatenate([made[n + h][1] for h in range(4)], axis=0)
        turned = lax.dot_general(
            eye, four, (((1,), (1,)), ((), ())), preferred_element_type=f32
        )
        for h in range(4):
            block = turned[:, (h // 2) * TILE : (h // 2 + 1) * TILE]
            block = jnp.where(upper, block, 0.0) if h % 2 else jnp.where(upper, 0.0, block)
            a_out[first + n + h] = block.astype(bf16)
            p_out[first + n + h] = made[n + h][2]


def take(src, idx):
    return jnp.take_along_axis(src, idx, axis=1, mode="promise_in_bounds")


def pair_sums(order, blocks, lists, a, b, p, join, own_tiles, tiles_ext):
    def step(first, tiles, carry):
        for h in range(tiles):
            u = order[first + h]
            m = u // own_tiles
            t = u - m * own_tiles
            held = b[u]
            acc = jnp.zeros((16, 2 * TILE), f32)
            for k in range(PARTNERS):
                q = m * tiles_ext + lists[m, k, t]
                both = jnp.dot(a[q], held, preferred_element_type=f32)
                reach = both[:, TILE:]
                inv = pltpu.reciprocal(both[:, :TILE], approx=True)
                ratio = reach * inv
                cubed = ratio * ratio * ratio
                sixth = cubed * cubed
                energy = sixth - cubed
                coeff = (energy + sixth) * inv
                high = coeff.astype(bf16)
                low = (coeff - high.astype(f32)).astype(bf16)
                left = jnp.concatenate([high, low], axis=0)
                right = jnp.concatenate([energy.astype(bf16), jnp.zeros((TILE, TILE), bf16)], axis=0)
                weights = p[q]
                acc += jnp.dot(
                    jnp.concatenate([weights, weights], axis=1),
                    jnp.concatenate([left, right], axis=1),
                    preferred_element_type=f32,
                )
            joined = acc[0:4] + acc[4:8] + acc[8:12]
            join[u] = jnp.concatenate([joined[:, :TILE], joined[:, TILE:]], axis=0)
        return carry

    pairs = blocks // 2
    lax.fori_loop(0, pairs, lambda n, c: step(n * (2 * BLOCK), 2 * BLOCK, c), 0)
    lax.fori_loop(2 * pairs, blocks, lambda n, c: step(n * BLOCK, BLOCK, c), 0)


def table(values):
    wide = jnp.concatenate([values[...], jnp.zeros_like(values[...])], axis=1)
    return jnp.broadcast_to(wide, (8, TILE))


def prep_kernel(coords_in, types, feats, first, last, place):
    images = feats.shape[1]
    slab, image = lax.axis_index("space"), lax.axis_index("image")
    place[0] = (slab > 0).astype(jnp.int32)
    place[1] = (slab < lax.axis_size("space") - 1).astype(jnp.int32)
    place[2] = (image == 0).astype(jnp.int32)
    place[3] = (image == lax.axis_size("image") - 1).astype(jnp.int32)
    for n in range(types.shape[0] // 8):
        kind = types[8 * n : 8 * n + 8].astype(f32)
        for h in range(8):
            t = 8 * n + h
            feats[3, :, t * TILE : (t + 1) * TILE] = jnp.broadcast_to(
                kind[h : h + 1], (images, TILE)
            )
    for c in range(3):
        rows = coords_in[c]
        feats[c] = rows
        first[c] = rows[0:1]
        last[c] = rows[images - 1 : images]


def own_kernel(
    lists, place, coords, types, well, radius,
    a, b, p, join, center, depth_s, order, count,
    near, radius_s,
):
    images = coords.shape[1]
    own_tiles = types.shape[0]
    tiles_ext = a.shape[0] // images
    wells, radii = table(well), table(radius)
    for n in range(own_tiles // 8):
        kind = types[8 * n : 8 * n + 8]
        depth_s[8 * n : 8 * n + 8] = take(wells, kind)
        radius_s[8 * n : 8 * n + 8] = take(radii, kind)
    for c in range(3):
        total = coords[c, :, 0:TILE]
        for t in range(1, own_tiles):
            total = total + coords[c, :, t * TILE : (t + 1) * TILE]
        middle = jnp.sum(total, axis=1, keepdims=True) * (1.0 / (own_tiles * TILE))
        for m in range(images):
            center[m, c : c + 1] = jnp.broadcast_to(middle[m : m + 1], (1, TILE))

    n_near, n_far = jnp.int32(0), jnp.int32(0)
    for m in range(images):
        middle = [repeated(center[m, c : c + 1]) for c in range(3)]

        def build(n, carry):
            n_near, n_far = carry
            made = []
            for h in range(OWN_BUILD):
                t = OWN_BUILD * n + h
                u = m * own_tiles + t
                xyz = [repeated(coords[c, m : m + 1, lanes(t)]) - middle[c] for c in range(3)]
                made.append(
                    streamed_features(
                        *xyz, repeated(depth_s[pl.ds(t, 1)]), repeated(radius_s[pl.ds(t, 1)])
                    )
                )
                b[u] = held_features(made[-1][0])
                last = lists[m, 0, t]
                for k in range(1, PARTNERS):
                    last = jnp.maximum(last, lists[m, k, t])
                inside = (last < own_tiles).astype(jnp.int32)
                near[n_near] = u
                order[n_far] = u
                n_near = n_near + inside
                n_far = n_far + (1 - inside)
            store_tiles(a, p, m * tiles_ext + OWN_BUILD * n, made)
            return n_near, n_far

        n_near, n_far = lax.fori_loop(0, own_tiles // OWN_BUILD, build, (n_near, n_far))
    blocks = n_near // BLOCK

    def move(n, n_far):
        order[n_far] = near[n]
        return n_far + 1

    n_far = lax.fori_loop(blocks * BLOCK, n_near, move, n_far)
    count[0] = n_far // BLOCK
    pair_sums(near, blocks, lists, a, b, p, join, own_tiles, tiles_ext)


def rest_kernel(
    lists, place, order, count, coords, below, above, own_depth, well, radius, hidx, ref, restr, prev, nxt,
    center, b, a_in, p_in, join_in,
    force, slope, bending, sums, a, p, join,
    halo_x, depth_s, radius_s,
):
    images = coords.shape[1]
    own_tiles = own_depth.shape[0]
    tiles_ext = a.shape[0] // images
    halo_tiles = tiles_ext - own_tiles
    side_tiles = halo_tiles // 2
    wells, radii = table(well), table(radius)

    wanted = [(side, m) for side in range(2) for m in range(images)]
    low, high = [], []
    for side, m in wanted:
        idx = jnp.concatenate(
            [hidx[m, side : side + 1, q * TILE : (q + 1) * TILE] for q in range(side_tiles)],
            axis=0,
        )
        low.append(idx & (TILE - 1))
        high.append(idx >> 7)

    def gather_row(r, carry):
        out = []
        for n, (side, m) in enumerate(wanted):
            source = above if side else below
            hit = high[n] == r
            for c in range(4):
                wide = jnp.broadcast_to(source[c, m : m + 1, lanes(r)], (8, TILE))
                out.append(jnp.where(hit, take(wide, low[n]), carry[4 * n + c]))
        return tuple(out)

    zero = jnp.zeros((8, TILE), f32)
    found = lax.fori_loop(0, own_tiles, gather_row, (zero,) * (8 * images), unroll=16)
    for n, (side, m) in enumerate(wanted):
        spot = slice(side * side_tiles, (side + 1) * side_tiles)
        for c in range(3):
            halo_x[m, c, spot] = found[4 * n + c]
        kind = found[4 * n + 3].astype(jnp.int32)
        depth_s[m, spot] = take(wells, kind) * place[side].astype(f32)
        radius_s[m, spot] = take(radii, kind)

    for m in range(images):
        middle = [repeated(center[m, c : c + 1]) for c in range(3)]

        def build(n, carry):
            made = []
            for h in range(BUILD):
                t = BUILD * n + h
                xyz = [repeated(halo_x[m, c, pl.ds(t, 1)]) - middle[c] for c in range(3)]
                made.append(
                    streamed_features(
                        *xyz, repeated(depth_s[m, pl.ds(t, 1)]), repeated(radius_s[m, pl.ds(t, 1)])
                    )
                )
            store_tiles(a, p, m * tiles_ext + own_tiles + BUILD * n, made)
            return carry

        lax.fori_loop(0, halo_tiles // BUILD, build, 0)

    pair_sums(order, count[0], lists, a, b, p, join, own_tiles, tiles_ext)

    def finish(n, carry):
        carry = list(carry)
        for h in range(16):
            t = 16 * n + h
            at = lanes(t)
            depth = own_depth[pl.ds(t, 1)]
            stiff = restr[:, at]
            rows = [join[m * own_tiles + t] for m in range(images)]
            weight = jnp.concatenate([r[0:1] for r in rows], axis=0)
            carry[5] += 2.0 * depth * jnp.concatenate([r[4:5] for r in rows], axis=0)
            for c in range(3):
                x = coords[c, :, at]
                middle = jnp.concatenate([center[m, c : c + 1] for m in range(images)], axis=0)
                moved = jnp.concatenate([r[1 + c : 2 + c] for r in rows], axis=0)
                offset = x - ref[c : c + 1, at]
                pull = stiff * offset
                total = 24.0 * depth * ((x - middle) * weight - moved) - pull
                force[c, :, at] = total
                before = jnp.concatenate([prev[c, :, at], x[0:1]], axis=0)
                after = jnp.concatenate([x[1:2], nxt[c, :, at]], axis=0)
                ahead, behind = after - x, x - before
                both_ways, bend = ahead + behind, ahead - behind
                slope[c, :, at] = both_ways
                bending[c, :, at] = bend
                carry[0] += both_ways * both_ways
                carry[1] += both_ways * bend
                carry[2] += bend * bend
                carry[3] += total * both_ways
                carry[4] += total * bend
                carry[5] += 0.5 * pull * offset
        return tuple(carry)

    zero = jnp.zeros((images, TILE), f32)
    line = lax.fori_loop(0, own_tiles // 16, finish, (zero,) * 6)
    line = jnp.concatenate(list(line) + [jnp.zeros((16 - 6 * images, TILE), f32)], axis=0)
    row, lane = rows_of((16, 16)), lax.broadcasted_iota(jnp.int32, (16, 16), 1)
    totals = jnp.sum(line, axis=1, keepdims=True)
    totals = jnp.sum(jnp.where(row == lane, totals, 0.0), axis=0, keepdims=True)
    sums[...] = jnp.broadcast_to(totals, (16, 16))


def band_kernel(place, shares, force, slope, bending, out, energies):
    total = jnp.sum(shares[...], axis=0, keepdims=True)
    images, atoms = force.shape[1], force.shape[2]
    parts = []
    for m in range(images):
        s_sq, cross, b_sq, f_s, f_b, energy = [
            total[:, images * n + m : images * n + m + 1] for n in range(6)
        ]
        energies[m] = (energy / (16 * atoms))[0, 0]
        base = 0.25 * (s_sq + b_sq) + small_eps
        ahead_sq, behind_sq = base + 0.5 * cross, base - 0.5 * cross
        ahead_len, behind_len = jnp.sqrt(ahead_sq), jnp.sqrt(behind_sq)
        inverse_sum = 1.0 / ahead_len + 1.0 / behind_len
        alpha = 0.5 * inverse_sum
        beta = -0.5 * cross / (ahead_sq * behind_sq * inverse_sum)
        tan_sq = alpha * alpha * s_sq + 2.0 * alpha * beta * cross + beta * beta * b_sq
        tan_len = jnp.sqrt(jnp.maximum(tan_sq, 0.0) + small_eps)
        along = (alpha * f_s + beta * f_b) / tan_len
        stretch = cross / (ahead_len + behind_len)
        gain = (spring_k * stretch - along) / tan_len
        gain = jnp.where(place[2 + m] == 1, 0.0, gain)
        parts.append((gain * alpha, gain * beta))
    for_s = jnp.concatenate([jnp.broadcast_to(q[0], (1, TILE)) for q in parts], axis=0)
    for_b = jnp.concatenate([jnp.broadcast_to(q[1], (1, TILE)) for q in parts], axis=0)
    for t in range(atoms // TILE):
        at = slice(t * TILE, (t + 1) * TILE)
        for c in range(3):
            out[c, :, at] = force[c, :, at] + for_s * slope[c, :, at] + for_b * bending[c, :, at]


def ring(axis, step):
    n = lax.axis_size(axis)
    return [(i, (i + step) % n) for i in range(n)]


def shape(dims, dtype=f32):
    return jax.ShapeDtypeStruct(dims, dtype)


def params(mib, **more):
    return dict(compiler_params=pltpu.CompilerParams(vmem_limit_bytes=mib << 20), **more)


def body(
    coords, ref_coords, restraint, atom_types, well_table, radius_table, tile_lists, halo_index
):
    images, _, atoms = coords.shape
    tiles = atoms // TILE
    tiles_ext = tiles + 2 * halo_index.shape[2] // TILE
    types = atom_types.reshape(tiles, TILE)
    well, radius = well_table[None], radius_table[None]
    feats, first, last, place = pl.pallas_call(
        prep_kernel,
        out_shape=(
            shape((4, images, atoms)),
            shape((3, 1, atoms)),
            shape((3, 1, atoms)),
            shape((4,), jnp.int32),
        ),
        in_specs=[VMEM] * 2,
        out_specs=(VMEM,) * 3 + (SMEM,),
        cost_estimate=pl.CostEstimate(flops=10**10, bytes_accessed=10**6, transcendentals=0),
        name="prep",
        **params(8),
    )(coords.transpose(1, 0, 2), types)
    below = lax.ppermute(feats, "space", ring("space", 1))
    above = lax.ppermute(feats, "space", ring("space", -1))
    prev = lax.ppermute(last, "image", ring("image", 1))
    nxt = lax.ppermute(first, "image", ring("image", -1))
    own = images * tiles
    a, b, p, join, center, depth, order, count = pl.pallas_call(
        own_kernel,
        out_shape=(
            shape((images * tiles_ext, TILE, TILE), bf16),
            shape((own, TILE, 2 * TILE), bf16),
            shape((images * tiles_ext, 16, TILE), bf16),
            shape((own, 8, TILE)),
            shape((images, 8, TILE)),
            shape((tiles, TILE)),
            shape((own,), jnp.int32),
            shape((1,), jnp.int32),
        ),
        in_specs=[SMEM] * 2 + [VMEM] * 4,
        out_specs=(VMEM,) * 6 + (SMEM,) * 2,
        scratch_shapes=[
            pltpu.SMEM((own,), jnp.int32),
            pltpu.VMEM((tiles, TILE), f32),
        ],
        cost_estimate=pl.CostEstimate(flops=60 * 10**9, bytes_accessed=10**6, transcendentals=0),
        name="own",
        **params(16),
    )(tile_lists, place, feats, types, well, radius)
    force, slope, bending, sums, *_ = pl.pallas_call(
        rest_kernel,
        out_shape=(
            shape((3, images, atoms)),
            shape((3, images, atoms)),
            shape((3, images, atoms)),
            shape((16, 16)),
            shape(a.shape, bf16),
            shape(p.shape, bf16),
            shape(join.shape),
        ),
        in_specs=[SMEM] * 4 + [VMEM] * 16,
        out_specs=(VMEM,) * 7,
        input_output_aliases={17: 4, 18: 5, 19: 6},
        scratch_shapes=[
            pltpu.VMEM((images, 3, tiles_ext - tiles, TILE), f32),
            pltpu.VMEM((images, tiles_ext - tiles, TILE), f32),
            pltpu.VMEM((images, tiles_ext - tiles, TILE), f32),
        ],
        name="rest",
        **params(16),
    )(
        tile_lists, place, order, count, feats, below, above, depth, well, radius, halo_index,
        ref_coords, restraint[None], prev, nxt, center, b, a, p, join,
    )
    shares = lax.all_to_all(sums, "space", 0, 0, tiled=True)
    out, energies = pl.pallas_call(
        band_kernel,
        out_shape=(shape((3, images, atoms)), shape((images,))),
        in_specs=[SMEM] + [VMEM] * 4,
        out_specs=(VMEM, SMEM),
        name="band",
        **params(8),
    )(place, shares, force, slope, bending)
    return out.transpose(1, 0, 2), energies


def solution(mesh):
    in_specs = (
        P("image", None, "space"),
        P(None, "space"),
        P("space"),
        P("space"),
        P(),
        P(),
        P("image", None, "space"),
        P("image", None, "space"),
    )
    out_specs = (P("image", None, "space"), P("image"))
    return jax.shard_map(body, mesh=mesh, in_specs=in_specs, out_specs=out_specs, check_vma=False)
```

```python
import jax
import jax.numpy as jnp
from jax import lax
from jax.experimental import pallas as pl
from jax.experimental.pallas import tpu as pltpu
from jax.sharding import PartitionSpec as P

TILE = 128
PARTNERS = 4
BLOCK = 16
BUILD = 16
OWN_BUILD = 64
spring_k = 2.0
small_eps = 1e-06
f32, bf16 = jnp.float32, jnp.bfloat16
GROUPS = ((0, 0), (0, 1), (1, 0), (0, 2), (2, 0), (1, 1))
VMEM = pl.BlockSpec(memory_space=pltpu.VMEM)
SMEM = pl.BlockSpec(memory_space=pltpu.SMEM)


def lanes(tile):
    return pl.ds(pl.multiple_of(tile * TILE, TILE), TILE)


def pieces(v):
    first = v.astype(bf16).astype(f32)
    rest = v - first
    second = rest.astype(bf16).astype(f32)
    return first, second, (rest - second).astype(bf16).astype(f32)


def rows_of(shape):
    return lax.broadcasted_iota(jnp.int32, shape, 0)


def streamed_features(x, y, z, depth, radius):
    row = rows_of((8, TILE))
    rr = radius * radius
    norm = x * x + y * y + z * z + rr
    base = jnp.where(row == 3, radius, jnp.where(row < 6, norm, rr))
    cut = pieces(jnp.where(row == 0, x, jnp.where(row == 1, y, jnp.where(row == 2, z, base))))
    ones = [jnp.where((row == 5) | (row == 7), 1.0, c) for c in cut]
    streamed = jnp.concatenate([ones[a] for a, _ in GROUPS], axis=0).astype(bf16)
    streamed = jnp.concatenate([streamed, jnp.zeros((16, TILE), bf16)], axis=0)
    quarter = row & 3
    moved = jnp.where(quarter == 0, 1.0, jnp.where(quarter == 1, x, jnp.where(quarter == 2, y, z)))
    p1, p2, p3 = pieces(depth * moved)
    weights = jnp.concatenate(
        [jnp.where(row < 4, p1, p2), jnp.where(row < 4, p3, 0.0)], axis=0
    ).astype(bf16)
    return cut, streamed, weights


def repeated(row):
    return jnp.broadcast_to(row, (8, TILE))


def held_features(cut):
    row = rows_of((8, TILE))
    blocks = []
    for a, b in GROUPS:
        own = 1.0 if (a, b) in ((0, 0), (0, 1), (0, 2)) else 0.0
        other = 1.0 if (a, b) in ((0, 0), (1, 0), (2, 0)) else 0.0
        scale_d = jnp.where(row < 3, -2.0, jnp.where(row == 3, 2.0, jnp.where(row == 5, own, 0.0)))
        scale_r = jnp.where(row == 3, 2.0, jnp.where(row == 7, own, 0.0))
        dist = cut[b] * scale_d + jnp.where(row == 4, other, 0.0)
        reach = cut[b] * scale_r + jnp.where(row == 6, other, 0.0)
        blocks.append(jnp.concatenate([dist, reach], axis=1))
    held = jnp.concatenate(blocks, axis=0).astype(bf16)
    rest = jnp.zeros((16, 2 * TILE), bf16)
    return jnp.concatenate([held, rest, held, rest], axis=0)


def store_tiles(a_out, p_out, first, made):
    eye = (rows_of((TILE, TILE)) == lax.broadcasted_iota(jnp.int32, (TILE, TILE), 1)).astype(bf16)
    upper = lax.broadcasted_iota(jnp.int32, (TILE, TILE), 1) >= TILE // 2
    for n in range(0, len(made), 4):
        four = jnp.concatenate([made[n + h][1] for h in range(4)], axis=0)
        turned = lax.dot_general(
            eye, four, (((1,), (1,)), ((), ())), preferred_element_type=f32
        )
        for h in range(4):
            block = turned[:, (h // 2) * TILE : (h // 2 + 1) * TILE]
            block = jnp.where(upper, block, 0.0) if h % 2 else jnp.where(upper, 0.0, block)
            a_out[first + n + h] = block.astype(bf16)
            p_out[first + n + h] = made[n + h][2]


def take(src, idx):
    return jnp.take_along_axis(src, idx, axis=1, mode="promise_in_bounds")


def pair_sums(order, blocks, lists, a, b, p, join, own_tiles, tiles_ext):
    def step(first, tiles, carry):
        for h in range(tiles):
            u = order[first + h]
            m = u // own_tiles
            t = u - m * own_tiles
            held = b[u]
            acc = jnp.zeros((16, 2 * TILE), f32)
            for k in range(PARTNERS):
                q = m * tiles_ext + lists[m, k, t]
                both = jnp.dot(a[q], held, preferred_element_type=f32)
                reach = both[:, TILE:]
                inv = pltpu.reciprocal(both[:, :TILE], approx=True)
                ratio = reach * inv
                cubed = ratio * ratio * ratio
                sixth = cubed * cubed
                energy = sixth - cubed
                coeff = (energy + sixth) * inv
                high = coeff.astype(bf16)
                low = (coeff - high.astype(f32)).astype(bf16)
                left = jnp.concatenate([high, low], axis=0)
                right = jnp.concatenate([energy.astype(bf16), jnp.zeros((TILE, TILE), bf16)], axis=0)
                weights = p[q]
                acc += jnp.dot(
                    jnp.concatenate([weights, weights], axis=1),
                    jnp.concatenate([left, right], axis=1),
                    preferred_element_type=f32,
                )
            joined = acc[0:4] + acc[4:8] + acc[8:12]
            join[u] = jnp.concatenate([joined[:, :TILE], joined[:, TILE:]], axis=0)
        return carry

    pairs = blocks // 2
    lax.fori_loop(0, pairs, lambda n, c: step(n * (2 * BLOCK), 2 * BLOCK, c), 0)
    lax.fori_loop(2 * pairs, blocks, lambda n, c: step(n * BLOCK, BLOCK, c), 0)


def table(values):
    wide = jnp.concatenate([values[...], jnp.zeros_like(values[...])], axis=1)
    return jnp.broadcast_to(wide, (8, TILE))


def prep_kernel(coords_in, types, feats, first, last, place):
    images = feats.shape[1]
    slab, image = lax.axis_index("space"), lax.axis_index("image")
    place[0] = (slab > 0).astype(jnp.int32)
    place[1] = (slab < lax.axis_size("space") - 1).astype(jnp.int32)
    place[2] = (image == 0).astype(jnp.int32)
    place[3] = (image == lax.axis_size("image") - 1).astype(jnp.int32)
    for n in range(types.shape[0] // 8):
        kind = types[8 * n : 8 * n + 8].astype(f32)
        for h in range(8):
            t = 8 * n + h
            feats[3, :, t * TILE : (t + 1) * TILE] = jnp.broadcast_to(
                kind[h : h + 1], (images, TILE)
            )
    for c in range(3):
        rows = coords_in[c]
        feats[c] = rows
        first[c] = rows[0:1]
        last[c] = rows[images - 1 : images]


def own_kernel(
    lists, place, coords, types, well, radius,
    a, b, p, join, center, depth_s, order, count,
    near, radius_s,
):
    images = coords.shape[1]
    own_tiles = types.shape[0]
    tiles_ext = a.shape[0] // images
    wells, radii = table(well), table(radius)
    for n in range(own_tiles // 8):
        kind = types[8 * n : 8 * n + 8]
        depth_s[8 * n : 8 * n + 8] = take(wells, kind)
        radius_s[8 * n : 8 * n + 8] = take(radii, kind)
    for c in range(3):
        total = coords[c, :, 0:TILE]
        for t in range(1, own_tiles):
            total = total + coords[c, :, t * TILE : (t + 1) * TILE]
        middle = jnp.sum(total, axis=1, keepdims=True) * (1.0 / (own_tiles * TILE))
        for m in range(images):
            center[m, c : c + 1] = jnp.broadcast_to(middle[m : m + 1], (1, TILE))

    n_near, n_far = jnp.int32(0), jnp.int32(0)
    for m in range(images):
        middle = [repeated(center[m, c : c + 1]) for c in range(3)]

        def build(n, carry):
            n_near, n_far = carry
            made = []
            for h in range(OWN_BUILD):
                t = OWN_BUILD * n + h
                u = m * own_tiles + t
                xyz = [repeated(coords[c, m : m + 1, lanes(t)]) - middle[c] for c in range(3)]
                made.append(
                    streamed_features(
                        *xyz, repeated(depth_s[pl.ds(t, 1)]), repeated(radius_s[pl.ds(t, 1)])
                    )
                )
                b[u] = held_features(made[-1][0])
                last = lists[m, 0, t]
                for k in range(1, PARTNERS):
                    last = jnp.maximum(last, lists[m, k, t])
                inside = (last < own_tiles).astype(jnp.int32)
                near[n_near] = u
                order[n_far] = u
                n_near = n_near + inside
                n_far = n_far + (1 - inside)
            store_tiles(a, p, m * tiles_ext + OWN_BUILD * n, made)
            return n_near, n_far

        n_near, n_far = lax.fori_loop(0, own_tiles // OWN_BUILD, build, (n_near, n_far))
    blocks = n_near // BLOCK

    def move(n, n_far):
        order[n_far] = near[n]
        return n_far + 1

    n_far = lax.fori_loop(blocks * BLOCK, n_near, move, n_far)
    count[0] = n_far // BLOCK
    pair_sums(near, blocks, lists, a, b, p, join, own_tiles, tiles_ext)


def rest_kernel(
    lists, place, order, count, coords, below, above, own_depth, well, radius, hidx, ref, restr, prev, nxt,
    center, b, a_in, p_in, join_in,
    force, slope, bending, sums, a, p, join,
    halo_x, depth_s, radius_s,
):
    images = coords.shape[1]
    own_tiles = own_depth.shape[0]
    tiles_ext = a.shape[0] // images
    halo_tiles = tiles_ext - own_tiles
    side_tiles = halo_tiles // 2
    wells, radii = table(well), table(radius)

    wanted = [(side, m) for side in range(2) for m in range(images)]
    low, high = [], []
    for side, m in wanted:
        idx = jnp.concatenate(
            [hidx[m, side : side + 1, q * TILE : (q + 1) * TILE] for q in range(side_tiles)],
            axis=0,
        )
        low.append(idx & (TILE - 1))
        high.append(idx >> 7)

    def gather_row(r, carry):
        out = []
        for n, (side, m) in enumerate(wanted):
            source = above if side else below
            hit = high[n] == r
            for c in range(4):
                wide = jnp.broadcast_to(source[c, m : m + 1, lanes(r)], (8, TILE))
                out.append(jnp.where(hit, take(wide, low[n]), carry[4 * n + c]))
        return tuple(out)

    zero = jnp.zeros((8, TILE), f32)
    found = lax.fori_loop(0, own_tiles, gather_row, (zero,) * (8 * images), unroll=16)
    for n, (side, m) in enumerate(wanted):
        spot = slice(side * side_tiles, (side + 1) * side_tiles)
        for c in range(3):
            halo_x[m, c, spot] = found[4 * n + c]
        kind = found[4 * n + 3].astype(jnp.int32)
        depth_s[m, spot] = take(wells, kind) * place[side].astype(f32)
        radius_s[m, spot] = take(radii, kind)

    for m in range(images):
        middle = [repeated(center[m, c : c + 1]) for c in range(3)]

        def build(n, carry):
            made = []
            for h in range(BUILD):
                t = BUILD * n + h
                xyz = [repeated(halo_x[m, c, pl.ds(t, 1)]) - middle[c] for c in range(3)]
                made.append(
                    streamed_features(
                        *xyz, repeated(depth_s[m, pl.ds(t, 1)]), repeated(radius_s[m, pl.ds(t, 1)])
                    )
                )
            store_tiles(a, p, m * tiles_ext + own_tiles + BUILD * n, made)
            return carry

        lax.fori_loop(0, halo_tiles // BUILD, build, 0)

    pair_sums(order, count[0], lists, a, b, p, join, own_tiles, tiles_ext)

    def finish(n, carry):
        carry = list(carry)
        for h in range(16):
            t = 16 * n + h
            at = lanes(t)
            depth = own_depth[pl.ds(t, 1)]
            stiff = restr[:, at]
            rows = [join[m * own_tiles + t] for m in range(images)]
            weight = jnp.concatenate([r[0:1] for r in rows], axis=0)
            carry[5] += 2.0 * depth * jnp.concatenate([r[4:5] for r in rows], axis=0)
            for c in range(3):
                x = coords[c, :, at]
                middle = jnp.concatenate([center[m, c : c + 1] for m in range(images)], axis=0)
                moved = jnp.concatenate([r[1 + c : 2 + c] for r in rows], axis=0)
                offset = x - ref[c : c + 1, at]
                pull = stiff * offset
                total = 24.0 * depth * ((x - middle) * weight - moved) - pull
                force[c, :, at] = total
                before = jnp.concatenate([prev[c, :, at], x[0:1]], axis=0)
                after = jnp.concatenate([x[1:2], nxt[c, :, at]], axis=0)
                ahead, behind = after - x, x - before
                both_ways, bend = ahead + behind, ahead - behind
                slope[c, :, at] = both_ways
                bending[c, :, at] = bend
                carry[0] += both_ways * both_ways
                carry[1] += both_ways * bend
                carry[2] += bend * bend
                carry[3] += total * both_ways
                carry[4] += total * bend
                carry[5] += 0.5 * pull * offset
        return tuple(carry)

    zero = jnp.zeros((images, TILE), f32)
    line = lax.fori_loop(0, own_tiles // 16, finish, (zero,) * 6)
    line = jnp.concatenate(list(line) + [jnp.zeros((16 - 6 * images, TILE), f32)], axis=0)
    row, lane = rows_of((16, 16)), lax.broadcasted_iota(jnp.int32, (16, 16), 1)
    totals = jnp.sum(line, axis=1, keepdims=True)
    totals = jnp.sum(jnp.where(row == lane, totals, 0.0), axis=0, keepdims=True)
    sums[...] = jnp.broadcast_to(totals, (16, 16))


def band_kernel(place, shares, force, slope, bending, out, energies):
    total = jnp.sum(shares[...], axis=0, keepdims=True)
    images, atoms = force.shape[1], force.shape[2]
    parts = []
    for m in range(images):
        s_sq, cross, b_sq, f_s, f_b, energy = [
            total[:, images * n + m : images * n + m + 1] for n in range(6)
        ]
        energies[m] = (energy / (16 * atoms))[0, 0]
        base = 0.25 * (s_sq + b_sq) + small_eps
        ahead_sq, behind_sq = base + 0.5 * cross, base - 0.5 * cross
        ahead_len, behind_len = jnp.sqrt(ahead_sq), jnp.sqrt(behind_sq)
        inverse_sum = 1.0 / ahead_len + 1.0 / behind_len
        alpha = 0.5 * inverse_sum
        beta = -0.5 * cross / (ahead_sq * behind_sq * inverse_sum)
        tan_sq = alpha * alpha * s_sq + 2.0 * alpha * beta * cross + beta * beta * b_sq
        tan_len = jnp.sqrt(jnp.maximum(tan_sq, 0.0) + small_eps)
        along = (alpha * f_s + beta * f_b) / tan_len
        stretch = cross / (ahead_len + behind_len)
        gain = (spring_k * stretch - along) / tan_len
        gain = jnp.where(place[2 + m] == 1, 0.0, gain)
        parts.append((gain * alpha, gain * beta))
    for_s = jnp.concatenate([jnp.broadcast_to(q[0], (1, TILE)) for q in parts], axis=0)
    for_b = jnp.concatenate([jnp.broadcast_to(q[1], (1, TILE)) for q in parts], axis=0)
    for t in range(atoms // TILE):
        at = slice(t * TILE, (t + 1) * TILE)
        for c in range(3):
            out[c, :, at] = force[c, :, at] + for_s * slope[c, :, at] + for_b * bending[c, :, at]


def ring(axis, step):
    n = lax.axis_size(axis)
    return [(i, (i + step) % n) for i in range(n)]


def shape(dims, dtype=f32):
    return jax.ShapeDtypeStruct(dims, dtype)


def params(mib, **more):
    return dict(compiler_params=pltpu.CompilerParams(vmem_limit_bytes=mib << 20), **more)


def body(
    coords, ref_coords, restraint, atom_types, well_table, radius_table, tile_lists, halo_index
):
    images, _, atoms = coords.shape
    tiles = atoms // TILE
    tiles_ext = tiles + 2 * halo_index.shape[2] // TILE
    types = atom_types.reshape(tiles, TILE)
    well, radius = well_table[None], radius_table[None]
    feats, first, last, place = pl.pallas_call(
        prep_kernel,
        out_shape=(
            shape((4, images, atoms)),
            shape((3, 1, atoms)),
            shape((3, 1, atoms)),
            shape((4,), jnp.int32),
        ),
        in_specs=[VMEM] * 2,
        out_specs=(VMEM,) * 3 + (SMEM,),
        cost_estimate=pl.CostEstimate(flops=10**10, bytes_accessed=10**6, transcendentals=0),
        name="prep",
        **params(8),
    )(coords.transpose(1, 0, 2), types)
    below = lax.ppermute(feats, "space", ring("space", 1))
    above = lax.ppermute(feats, "space", ring("space", -1))
    prev = lax.ppermute(last, "image", ring("image", 1))
    nxt = lax.ppermute(first, "image", ring("image", -1))
    own = images * tiles
    a, b, p, join, center, depth, order, count = pl.pallas_call(
        own_kernel,
        out_shape=(
            shape((images * tiles_ext, TILE, TILE), bf16),
            shape((own, TILE, 2 * TILE), bf16),
            shape((images * tiles_ext, 16, TILE), bf16),
            shape((own, 8, TILE)),
            shape((images, 8, TILE)),
            shape((tiles, TILE)),
            shape((own,), jnp.int32),
            shape((1,), jnp.int32),
        ),
        in_specs=[SMEM] * 2 + [VMEM] * 4,
        out_specs=(VMEM,) * 6 + (SMEM,) * 2,
        scratch_shapes=[
            pltpu.SMEM((own,), jnp.int32),
            pltpu.VMEM((tiles, TILE), f32),
        ],
        cost_estimate=pl.CostEstimate(flops=60 * 10**9, bytes_accessed=10**6, transcendentals=0),
        name="own",
        **params(16),
    )(tile_lists, place, feats, types, well, radius)
    force, slope, bending, sums, *_ = pl.pallas_call(
        rest_kernel,
        out_shape=(
            shape((3, images, atoms)),
            shape((3, images, atoms)),
            shape((3, images, atoms)),
            shape((16, 16)),
            shape(a.shape, bf16),
            shape(p.shape, bf16),
            shape(join.shape),
        ),
        in_specs=[SMEM] * 4 + [VMEM] * 16,
        out_specs=(VMEM,) * 7,
        input_output_aliases={17: 4, 18: 5, 19: 6},
        scratch_shapes=[
            pltpu.VMEM((images, 3, tiles_ext - tiles, TILE), f32),
            pltpu.VMEM((images, tiles_ext - tiles, TILE), f32),
            pltpu.VMEM((images, tiles_ext - tiles, TILE), f32),
        ],
        name="rest",
        **params(16),
    )(
        tile_lists, place, order, count, feats, below, above, depth, well, radius, halo_index,
        ref_coords, restraint[None], prev, nxt, center, b, a, p, join,
    )
    shares = lax.all_to_all(sums, "space", 0, 0, tiled=True)
    out, energies = pl.pallas_call(
        band_kernel,
        out_shape=(shape((3, images, atoms)), shape((images,))),
        in_specs=[SMEM] + [VMEM] * 4,
        out_specs=(VMEM, SMEM),
        name="band",
        **params(8),
    )(place, shares, force, slope, bending)
    return out.transpose(1, 0, 2), energies


def solution(mesh):
    in_specs = (
        P("image", None, "space"),
        P(None, "space"),
        P("space"),
        P("space"),
        P(),
        P(),
        P("image", None, "space"),
        P("image", None, "space"),
    )
    out_specs = (P("image", None, "space"), P("image"))
    return jax.shard_map(body, mesh=mesh, in_specs=in_specs, out_specs=out_specs, check_vma=False)
```
